32 devices in a mesh: grp: 2 (over x), row: 16 (over z, y, core).
Axes of the slice: x: 2, y: 2, z: 4, core: 2. Of those that a mesh axis runs over, the one named last changes fastest.
Arguments:
- node_feats: bfloat16 [512, 256], P(('grp', 'row')), parts along dimension 0, may hold values from -6 to 6
- pair_feats: bfloat16 [512, 256, 128], P(('grp', 'row')), parts along dimension 0, may hold values from -6 to 6
- trans: bfloat16 [512, 3], P(('grp', 'row')), parts along dimension 0, may hold values from -4 to 4
- frame_seed: int32 [512, 3], P(('grp', 'row')), parts along dimension 0, may hold values from 0 to 255
- residue_mask: int32 [512], P('grp'), parts along dimension 0, may hold values 0 or 1
- chain_index: int32 [512], P('grp'), parts along dimension 0, may hold values from 0 to 7, never falling along the last dimension, each value on 1 to 64 neighbouring positions
- w_qkv: bfloat16 [256, 576], replicated, may hold values from -0.375 to 0.375
- w_points: bfloat16 [256, 576], replicated, may hold values from -0.375 to 0.375
- w_bias: bfloat16 [128, 12], replicated, may hold values from -0.5 to 0.5
- head_weights: float32 [12], replicated, may hold values from -2 to 1
- chain_bias: float32 [12], replicated, may hold values from -6 to 6
- w_out: bfloat16 [2112, 256], replicated, may hold values from -0.125 to 0.125
- b_out: float32 [256], replicated, may hold values from -3 to 3
- w_trans: bfloat16 [3, 256, 256], replicated, may hold values from -0.375 to 0.375
- w_edge_node: bfloat16 [256, 128], replicated, may hold values from -0.375 to 0.375
- w_edge_in: bfloat16 [384, 384], replicated, may hold values from -0.3125 to 0.3125
- b_edge_in: float32 [384], replicated, may hold values from -3 to 3
- w_edge_mid: bfloat16 [384, 384], replicated, may hold values from -0.3125 to 0.3125
- b_edge_mid: float32 [384], replicated, may hold values from -3 to 3
- w_edge_out: bfloat16 [384, 128], replicated, may hold values from -0.3125 to 0.3125
- b_edge_out: float32 [128], replicated, may hold values from -3 to 3
Outputs:
- node_out: bfloat16 [512, 256], P(('grp', 'row')), parts along dimension 0
- pair_out: bfloat16 [512, 256, 128], P(('grp', 'row')), parts along dimension 0
The draws below stay inside these ranges and needn't reach their ends.
There are 2 independent parts, one for each index of `grp`. The reference program is written for one: setup_inputs(seed, part) draws one part's arguments, and reference() takes and returns one part's arrays. A program takes and returns all parts, laid end to end along the dimension named above; an argument that names none is the same for every part. Nothing has to cross between parts.
Inputs may be any that keep to these rules, and one draw needn't show every extreme that they name: `chain_index`: never falls along the residues; a chain holds 1 to 64 residues.
All inputs are finite; a program needn't handle non-finite values.
Results may differ from the reference program's by a relative error of at most 0.013.
Values may be sent and summed in bfloat16 or wider, within the bound.
A program may use at most 64 MiB of HBM per device.

```python
import math
import jax
import jax.numpy as jnp
import numpy as np
from jax import lax

D_NODE = 256
C_PAIR = 128
HEADS = 12
HEAD_DIM = 16
QK_POINTS = 4
V_POINTS = 8
EDGE_NODE = 128
EDGE_HID = 384
CHAINS = 8
RES_DEV = 16
RES = 256


def set_ends(values, rng, smallest, top_value):
    extent = values.shape
    index_at = [jax.random.randint(jax.random.fold_in(rng, axis), (), 0, extent[axis]) for axis in range(len(extent))]
    values = values.at[tuple(index_at)].set(smallest)
    longest = extent.index(max(extent))
    index_at[longest] = (index_at[longest] + 1) % extent[longest]
    return values.at[tuple(index_at)].set(top_value)


def block_levels(stream_key, shape, pieces, low, largest):
    def one(position, blocks):
        heights = jax.random.uniform(jax.random.fold_in(jax.random.fold_in(stream_key, 6), position), (blocks,), jnp.float32, low / len(pieces), largest / len(pieces))
        return jnp.repeat(jnp.exp(heights), shape[position] // blocks).reshape((-1,) + (1,) * (len(shape) - position - 1))

    factor_of = one(*pieces[0])
    for cut in pieces[1:]:
        factor_of = factor_of * one(*cut)
    return factor_of


def profile(amount, total, reach, slope):
    portions = [(1 << 20) // math.isqrt(standing ** slope) + 1 for standing in range(2, amount + 1)]
    rest, given = total - reach - (amount - 1), [1] * (amount - 1)
    while rest > 0:
        free = [i for i in range(amount - 1) if given[i] < reach]
        mass, left = sum([portions[i] for i in free]), rest
        for i in free:
            extra = min(reach - given[i], max(1, left * portions[i] // mass), rest)
            given[i] = given[i] + extra
            rest = rest - extra
    return np.array([reach] + given)


def ragged_sizes(key, amount, total, limit, lean):
    if amount == 2:
        one = jax.random.randint(key, (), max(1, total - limit), min(limit, total - 1) + 1)
        return jnp.stack([one, total - one])
    sizes = jnp.asarray(profile(amount, total, limit, lean), jnp.int32)
    twos = (amount - 1) // 2
    source_of, taker = sizes[1:1 + 2 * twos:2], sizes[2:2 + 2 * twos:2]
    slack = jnp.minimum(source_of - 1, limit - taker)
    moved = jax.random.randint(jax.random.fold_in(key, 1), (twos,), 0, 1 << 20) % (slack + 1)
    sizes = sizes.at[1:1 + 2 * twos:2].set(source_of - moved).at[2:2 + 2 * twos:2].set(taker + moved)
    return sizes[jax.random.permutation(jax.random.fold_in(key, 2), amount)]


def bell_draw(own_key, dims, deviation, most, pieces=(), held_as=jnp.bfloat16):
    values = jax.random.normal(own_key, dims, jnp.float32) * deviation
    if len(pieces) > 0:
        values = block_levels(own_key, dims, pieces, -0.22, 0.18) * values
    return jnp.clip(values, min=-most, max=most).astype(held_as)


def setup_inputs(seed: int = 0, part: int = 0) -> dict:
    splits = jax.random.split(jax.random.key(seed), 22)
    part_splits = jax.random.split(jax.random.fold_in(splits[21], part), 22)
    return {
        "node_feats": bell_draw(part_splits[0], (RES, D_NODE), 1.0, 6.0, ((0, 16),)),
        "pair_feats": bell_draw(part_splits[1], (RES, RES, C_PAIR), 1.0, 6.0, ((0, 16),)),
        "trans": bell_draw(part_splits[2], (RES, 3), 1.0, 4.0, ((0, 16),)),
        "frame_seed": set_ends(jax.random.randint(part_splits[3], (RES, 3), 0, 256), jax.random.fold_in(part_splits[3], 1), 0, 255).astype(jnp.int32),
        "residue_mask": set_ends((jax.random.randint(part_splits[4], (RES,), 0, 8) < 7).astype(jnp.int32), jax.random.fold_in(part_splits[4], 1), 0, 1),
        "chain_index": jnp.searchsorted(jnp.cumsum(ragged_sizes(part_splits[5], CHAINS, RES, RES // 4, 2)), jnp.arange(RES), side="right").astype(jnp.int32),
        "w_qkv": bell_draw(splits[6], (D_NODE, 3 * HEADS * HEAD_DIM), D_NODE ** -0.5, 0.375),
        "w_points": bell_draw(splits[7], (D_NODE, 3 * HEADS * (2 * QK_POINTS + V_POINTS)), D_NODE ** -0.5, 0.375),
        "w_bias": bell_draw(splits[8], (C_PAIR, HEADS), C_PAIR ** -0.5, 0.5),
        "head_weights": jnp.clip(jax.random.uniform(splits[9], (HEADS,), jnp.float32, -2.0, 1.0), -2.0, 1.0),
        "chain_bias": jnp.clip(jax.random.uniform(splits[10], (HEADS,), jnp.float32, -6.0, 6.0), -6.0, 6.0),
        "w_out": bell_draw(splits[11], (HEADS * (HEAD_DIM + 4 * V_POINTS + C_PAIR), D_NODE), (HEADS * (HEAD_DIM + 4 * V_POINTS + C_PAIR)) ** -0.5, 0.125),
        "b_out": bell_draw(splits[12], (D_NODE,), 0.5, 3.0, (), jnp.float32),
        "w_trans": bell_draw(splits[13], (3, D_NODE, D_NODE), D_NODE ** -0.5, 0.375),
        "w_edge_node": bell_draw(splits[14], (D_NODE, EDGE_NODE), D_NODE ** -0.5, 0.375),
        "w_edge_in": bell_draw(splits[15], (EDGE_HID, EDGE_HID), EDGE_HID ** -0.5, 0.3125),
        "b_edge_in": bell_draw(splits[16], (EDGE_HID,), 0.5, 3.0, (), jnp.float32),
        "w_edge_mid": bell_draw(splits[17], (EDGE_HID, EDGE_HID), EDGE_HID ** -0.5, 0.3125),
        "b_edge_mid": bell_draw(splits[18], (EDGE_HID,), 0.5, 3.0, (), jnp.float32),
        "w_edge_out": bell_draw(splits[19], (EDGE_HID, C_PAIR), EDGE_HID ** -0.5, 0.3125),
        "b_edge_out": bell_draw(splits[20], (C_PAIR,), 0.5, 3.0, (), jnp.float32),
    }


mask_bias = 100000.0
norm_eps = 1e-05
point_eps = 1e-08

def rotations(frame_seed):
    angles = frame_seed.astype(jnp.float32) * (2.0 * math.pi / 256.0)
    cosine = jnp.cos(angles)
    sine = jnp.sin(angles)
    zeros = jnp.zeros_like(cosine[:, 0])
    ones = jnp.ones_like(cosine[:, 0])

    def about_z(index):
        return jnp.stack([jnp.stack([cosine[:, index], -sine[:, index], zeros], -1), jnp.stack([sine[:, index], cosine[:, index], zeros], -1), jnp.stack([zeros, zeros, ones], -1)], -2)
    about_y = jnp.stack([jnp.stack([cosine[:, 1], zeros, sine[:, 1]], -1), jnp.stack([zeros, ones, zeros], -1), jnp.stack([-sine[:, 1], zeros, cosine[:, 1]], -1)], -2)
    return jnp.einsum('nab,nbc,ncd->nad', about_z(0), about_y, about_z(2), precision=lax.Precision.HIGHEST)

def project_nodes(nodes, trans, rotate, w_plain, w_spatial):
    plain = jnp.dot(nodes, w_plain, preferred_element_type=jnp.float32).astype(jnp.bfloat16)
    local = jnp.dot(nodes, w_spatial, preferred_element_type=jnp.float32).reshape(nodes.shape[0], 3, -1)
    spatial = jnp.einsum('nab,nbk->nak', rotate, local, precision=lax.Precision.HIGHEST)
    spatial = spatial + trans.astype(jnp.float32)[:, :, None]
    return (plain, spatial.astype(jnp.bfloat16))

def layer_norm(values):
    centred = values - lax.optimization_barrier(jnp.mean(values, -1, keepdims=True))
    return centred / jnp.sqrt(lax.optimization_barrier(jnp.mean(centred * centred, -1, keepdims=True)) + norm_eps)

def scores(query, qpoints, pair_block, key, kpoints, mask_q, mask_k, chain_q, chain_k, w_bias, head_weights, chain_bias):
    head_dim = query.shape[-1]
    qk_points = qpoints.shape[-1]
    dots = jnp.einsum('bhc,mhc->hbm', query.astype(jnp.float32), key.astype(jnp.float32))
    bias = jnp.einsum('bmc,ch->hbm', pair_block.astype(jnp.float32), w_bias.astype(jnp.float32))
    qfloat = qpoints.astype(jnp.float32)
    kfloat = kpoints.astype(jnp.float32)
    cross = jnp.einsum('bahp,mahp->hbm', qfloat, kfloat, precision=lax.Precision.HIGHEST)
    qsquare = lax.optimization_barrier(jnp.sum(qfloat * qfloat, axis=(1, 3))).T
    ksquare = lax.optimization_barrier(jnp.sum(kfloat * kfloat, axis=(1, 3))).T
    distance = qsquare[:, :, None] + ksquare[:, None, :] - 2.0 * cross
    gamma = jax.nn.softplus(head_weights)
    weight_c = math.sqrt(2.0 / (9.0 * qk_points))
    same = (chain_q[:, None] == chain_k[None, :]).astype(jnp.float32)
    pair_mask = (mask_q[:, None] * mask_k[None, :]).astype(jnp.float32)
    logit = math.sqrt(1.0 / 3.0) * (dots / math.sqrt(head_dim) + bias - 0.5 * weight_c * gamma[:, None, None] * distance)
    return logit + chain_bias[:, None, None] * same[None] + mask_bias * (pair_mask[None] - 1.0)

def update_nodes(nodes, node_part, point_part, pair_part, rotate, trans, mask_q, w_out, b_out, w_trans):
    count = nodes.shape[0]
    shifted = point_part - trans.astype(jnp.float32)[:, :, None, None]
    local = jnp.einsum('bca,bchp->bahp', rotate, shifted, precision=lax.Precision.HIGHEST)
    length = jnp.sqrt(lax.optimization_barrier(jnp.sum(local * local, 1)) + point_eps)
    joined = jnp.concatenate([node_part.reshape(count, -1), local.reshape(count, -1), length.reshape(count, -1), pair_part.reshape(count, -1)], -1).astype(jnp.bfloat16)
    update = jnp.dot(joined, w_out, preferred_element_type=jnp.float32) + b_out
    first = layer_norm(nodes.astype(jnp.float32) + update).astype(jnp.bfloat16)
    hidden = jax.nn.relu(jnp.dot(first, w_trans[0], preferred_element_type=jnp.float32)).astype(jnp.bfloat16)
    hidden = jax.nn.relu(jnp.dot(hidden, w_trans[1], preferred_element_type=jnp.float32)).astype(jnp.bfloat16)
    last = jnp.dot(hidden, w_trans[2], preferred_element_type=jnp.float32)
    return (layer_norm(first.astype(jnp.float32) + last) * mask_q.astype(jnp.float32)[:, None]).astype(jnp.bfloat16)

def reference(node_feats, pair_feats, trans, frame_seed, residue_mask, chain_index, w_qkv, w_points, w_bias, head_weights, chain_bias, w_out, b_out, w_trans, w_edge_node, w_edge_in, b_edge_in, w_edge_mid, b_edge_mid, w_edge_out, b_edge_out):
    width = HEADS * HEAD_DIM
    rotate = rotations(frame_seed)
    plain, spatial = project_nodes(node_feats, trans, rotate, w_qkv, w_points)
    spatial = spatial.reshape(RES, 3, HEADS, 2 * QK_POINTS + V_POINTS)
    query = plain[:, :width].reshape(RES, HEADS, HEAD_DIM)
    key = plain[:, width:2 * width].reshape(RES, HEADS, HEAD_DIM)
    value = plain[:, 2 * width:].reshape(RES, HEADS, HEAD_DIM)
    qpoints = spatial[..., :QK_POINTS]
    kpoints = spatial[..., QK_POINTS:2 * QK_POINTS]
    vpoints = spatial[..., 2 * QK_POINTS:]
    starts = jnp.arange(RES // RES_DEV, dtype=jnp.int32) * RES_DEV

    def take(array, start):
        return lax.dynamic_slice_in_dim(array, start, RES_DEV, 0)

    def attend_block(start):
        pair_block = take(pair_feats, start)
        logit = scores(take(query, start), take(qpoints, start), pair_block, key, kpoints, take(residue_mask, start), residue_mask, take(chain_index, start), chain_index, w_bias, head_weights, chain_bias)
        expo = jnp.exp(logit - lax.optimization_barrier(jnp.max(logit, 2, keepdims=True)))
        total = lax.optimization_barrier(jnp.sum(expo, 2)).T
        weights = lax.optimization_barrier(expo.astype(jnp.bfloat16)).astype(jnp.float32)
        node_part = jnp.einsum('hbm,mhc->bhc', weights, value.astype(jnp.float32)) / total[:, :, None]
        point_part = jnp.einsum('hbm,mahp->bahp', weights, vpoints.astype(jnp.float32)) / total[:, None, :, None]
        pair_part = jnp.einsum('hbm,bmc->bhc', weights, pair_block.astype(jnp.float32)) / total[:, :, None]
        return update_nodes(take(node_feats, start), node_part, point_part, pair_part, take(rotate, start), take(trans, start), take(residue_mask, start), w_out, b_out, w_trans)
    node_out = lax.map(attend_block, starts).reshape(RES, D_NODE)
    endpoint = jnp.dot(node_out, w_edge_node, preferred_element_type=jnp.float32).astype(jnp.bfloat16)
    near = jnp.dot(endpoint, w_edge_in[C_PAIR:C_PAIR + EDGE_NODE], preferred_element_type=jnp.float32) + b_edge_in
    far = jnp.dot(endpoint, w_edge_in[C_PAIR + EDGE_NODE:], preferred_element_type=jnp.float32)
    mask_all = residue_mask.astype(jnp.float32)

    def edge_block(start):
        pair_block = take(pair_feats, start)
        cells = RES_DEV * RES
        pre = jnp.dot(pair_block.reshape(cells, C_PAIR), w_edge_in[:C_PAIR], preferred_element_type=jnp.float32)
        pre = pre.reshape(RES_DEV, RES, EDGE_HID) + take(near, start)[:, None, :] + far[None]
        first = jax.nn.relu(pre).astype(jnp.bfloat16).reshape(cells, EDGE_HID)
        second = jax.nn.relu(jnp.dot(first, w_edge_mid, preferred_element_type=jnp.float32) + b_edge_mid)
        own = take(endpoint, start)
        joined = jnp.concatenate([pair_block, jnp.broadcast_to(own[:, None, :], (RES_DEV, RES, EDGE_NODE)), jnp.broadcast_to(endpoint[None], (RES_DEV, RES, EDGE_NODE))], -1)
        resid = (second + joined.reshape(cells, EDGE_HID).astype(jnp.float32)).astype(jnp.bfloat16)
        out = jnp.dot(resid, w_edge_out, preferred_element_type=jnp.float32) + b_edge_out
        pair_mask = take(mask_all, start)[:, None] * mask_all[None, :]
        return (layer_norm(out).reshape(RES_DEV, RES, C_PAIR) * pair_mask[:, :, None]).astype(jnp.bfloat16)
    pair_out = lax.map(edge_block, starts).reshape(RES, RES, C_PAIR)
    return (node_out, pair_out)
```

```python
import functools
import math

import jax
import jax.numpy as jnp
from jax import lax
from jax.experimental import pallas as pl
from jax.experimental.pallas import tpu as pltpu
from jax.sharding import PartitionSpec as P

C_PAIR = 128
HEADS = 12
HEAD_DIM = 16
QK_POINTS = 4
V_POINTS = 8
POINTS = 2 * QK_POINTS + V_POINTS
EDGE_NODE = 128
WIDTH = HEADS * HEAD_DIM
PACK = 16
FRAME = 128

mask_bias = 100000.0
norm_eps = 1e-05
point_eps = 1e-08
F32 = jnp.float32
BF16 = jnp.bfloat16
MESH = pl.DeviceIdType.MESH
VMEM_LIMIT = 60 << 20


def dot(a, b):
    return jnp.dot(a, b, preferred_element_type=F32)


def dot_nt(a, b):
    return lax.dot_general(a, b, (((1,), (1,)), ((), ())), preferred_element_type=F32)


def layer_norm(values):
    centred = values - jnp.mean(values, -1, keepdims=True)
    return centred * lax.rsqrt(jnp.mean(centred * centred, -1, keepdims=True) + norm_eps)


def cos_sin(steps):
    quarter = jnp.floor((steps + 32.0) * (1.0 / 64.0))
    x = (steps - 64.0 * quarter) * (2.0 * math.pi / 256.0)
    y = x * x
    c = 1.0 + y * (-0.5 + y * (1 / 24 + y * (-1 / 720 + y * (1 / 40320 - y * (1 / 3628800)))))
    s = x * (1.0 + y * (-1 / 6 + y * (1 / 120 + y * (-1 / 5040 + y * (1 / 362880)))))
    one, two, three = quarter == 1.0, quarter == 2.0, quarter == 3.0
    cosine = jnp.where(one, -s, jnp.where(two, -c, jnp.where(three, s, c)))
    sine = jnp.where(one, c, jnp.where(two, -s, jnp.where(three, -c, s)))
    return cosine, sine


def frames(frame):
    cosine, sine = cos_sin(frame)
    c0, c1, c2 = (cosine[:, k : k + 1] for k in (3, 4, 5))
    s0, s1, s2 = (sine[:, k : k + 1] for k in (3, 4, 5))
    rotate = (
        (c0 * c1 * c2 - s0 * s2, -c0 * c1 * s2 - s0 * c2, c0 * s1),
        (s0 * c1 * c2 + c0 * s2, c0 * c2 - s0 * c1 * s2, s0 * s1),
        (-s1 * c2, s1 * s2, c1),
    )
    return rotate, tuple(frame[:, k : k + 1] for k in range(3))


def spatial_points(nodes, rotate, trans, w_points):
    local = [dot(nodes, w_points[:, b * WIDTH : (b + 1) * WIDTH]) for b in range(3)]
    return [
        (
            rotate[a][0] * local[0] + rotate[a][1] * local[1] + rotate[a][2] * local[2] + trans[a]
        ).astype(BF16)
        for a in range(3)
    ]


def iota(shape, axis):
    return lax.broadcasted_iota(jnp.int32, shape, axis)


def node_kernel(
    n,
    packed,
    mask_ref,
    chain_ref,
    w_bias,
    head_weights,
    chain_bias,
    b_out,
    w_edge_node,
    pair_hbm,
    w_qkv_hbm,
    w_points_hbm,
    w_out_hbm,
    w_trans_hbm,
    node_out,
    ends_out,
    own_out,
    gathered,
    ends,
    own_end,
    pair,
    w_qkv,
    w_points,
    w_out,
    w_trans,
    bias,
    wide,
    w_local,
    pair_part,
    load_sem,
    send_a,
    recv_a,
    send_b,
    recv_b,
):
    me = lax.axis_index("row")
    rows = packed.shape[0]
    count = rows * n
    lines = rows * PACK

    barrier = pltpu.get_barrier_semaphore()

    def greet(s, carry):
        pl.semaphore_signal(
            barrier, inc=1, device_id={"row": lax.rem(me + s, n)}, device_id_type=MESH
        )
        return carry

    lax.fori_loop(1, n, greet, 0)
    loads = [
        pltpu.make_async_copy(src, dst, load_sem.at[k])
        for k, (src, dst) in enumerate(
            (
                (pair_hbm, pair),
                (w_qkv_hbm, w_qkv),
                (w_points_hbm, w_points),
                (w_out_hbm, w_out),
                (w_trans_hbm, w_trans),
            )
        )
    ]
    for load in loads:
        load.start()
    pl.semaphore_wait(barrier, n - 1)

    def copy_of(s, src, dst, send, recv):
        return pltpu.make_async_remote_copy(
            src_ref=src,
            dst_ref=dst.at[pl.ds(pl.multiple_of(me * rows, rows), rows)],
            send_sem=send.at[s],
            recv_sem=recv.at[s],
            device_id={"row": lax.rem(me + s, n)},
            device_id_type=MESH,
        )

    def exchange(src, dst, send, recv):
        def go(s, carry):
            copy_of(s, src, dst, send, recv).start()
            return carry

        lax.fori_loop(1, n, go, 0)

    def settle(src, dst, send, recv):
        def go(s, carry):
            copy_of(s, src, dst, send, recv).wait()
            return carry

        lax.fori_loop(1, n, go, 0)

    exchange(packed, gathered, send_a, recv_a)
    mine = pl.ds(pl.multiple_of(me * rows, rows), rows)
    gathered[mine, :] = packed[...]

    wide[...] = jnp.zeros_like(wide)
    wide[:, :HEADS] = w_bias[...].astype(F32)
    w_bias_t = wide[...].T[:PACK].astype(BF16)
    loads[0].wait()

    def bias_row(i, carry):
        bias[pl.ds(pl.multiple_of(i * PACK, PACK), PACK), :] = dot_nt(w_bias_t, pair[i])
        return carry

    lax.fori_loop(0, rows, bias_row, 0, unroll=4)

    line = iota((lines, 1), 0)
    line_head = line % PACK
    line_row = line // PACK
    at_own = iota((lines, count), 1) == me * rows + line_row
    chain_q = jnp.sum(jnp.where(at_own, chain_ref[...], 0), 1, keepdims=True)
    mask_q = jnp.sum(jnp.where(at_own, mask_ref[...], 0), 1, keepdims=True)
    at_head = iota((lines, HEADS), 1) == line_head
    gamma = jnp.sum(jnp.where(at_head, jax.nn.softplus(head_weights[...]), 0.0), 1, keepdims=True)
    chain_add = jnp.sum(jnp.where(at_head, chain_bias[...], 0.0), 1, keepdims=True)
    column = iota((lines, WIDTH), 1)
    of_head = column // HEAD_DIM == line_head
    of_key = of_head & (column % POINTS >= QK_POINTS) & (column % POINTS < 2 * QK_POINTS)
    of_value = of_head & (column % POINTS >= 2 * QK_POINTS)
    spread = (iota((lines, rows), 1) == line_row).astype(BF16)
    same = (chain_q == chain_ref[...]).astype(F32)
    pair_mask = (mask_q * mask_ref[...]).astype(F32)
    bias[...] = bias[...] * math.sqrt(1.0 / 3.0) + (
        chain_add * same + mask_bias * (pair_mask - 1.0)
    )

    loads[1].wait()
    loads[2].wait()
    nodes = packed[:, :-FRAME]
    rotate, trans = frames(packed[:, -FRAME:].astype(F32))
    query = dot(nodes, w_qkv[:, :WIDTH]).astype(BF16)
    own_points = spatial_points(nodes, rotate, trans, w_points)
    q_lines = jnp.where(of_head, dot(spread, query), 0.0).astype(BF16)
    p_lines = [
        jnp.where(of_key, pltpu.roll(dot(spread, own_points[a]), QK_POINTS, 1), 0.0)
        for a in range(3)
    ]
    q_square = sum(jnp.sum(p * p, 1, keepdims=True) for p in p_lines)
    p_lines = [(-2.0 * p).astype(BF16) for p in p_lines]
    ones_key = of_key.astype(BF16)

    loads[3].wait()
    for k in range(4):
        start = WIDTH + k * HEADS * V_POINTS
        block = w_out[start : start + HEADS * V_POINTS, :].astype(F32)
        block = block.reshape(HEADS, V_POINTS, -1)
        block = jnp.concatenate([jnp.zeros_like(block), block], 1)
        w_local[k] = block.reshape(WIDTH, -1).astype(BF16)

    settle(packed, gathered, send_a, recv_a)

    every = gathered[:, :-FRAME]
    key = dot(every, w_qkv[:, WIDTH : 2 * WIDTH]).astype(BF16)
    value = dot(every, w_qkv[:, 2 * WIDTH :]).astype(BF16)
    rotate_all, trans_all = frames(gathered[:, -FRAME:].astype(F32))
    points = spatial_points(every, rotate_all, trans_all, w_points)
    square = sum(p.astype(F32) * p.astype(F32) for p in points)
    high = square.astype(BF16)
    rest = square - high.astype(F32)
    middle = rest.astype(BF16)
    low = (rest - middle.astype(F32)).astype(BF16)
    dots = dot_nt(q_lines, key)
    distance = q_square + (
        dot_nt(p_lines[0], points[0])
        + dot_nt(p_lines[1], points[1])
        + dot_nt(p_lines[2], points[2])
        + dot_nt(ones_key, high)
        + dot_nt(ones_key, middle)
        + dot_nt(ones_key, low)
    )
    weight_c = math.sqrt(2.0 / (9.0 * QK_POINTS))
    third = math.sqrt(1.0 / 3.0)
    logit = (
        dots * (third / math.sqrt(HEAD_DIM)) - (0.5 * weight_c * third) * gamma * distance
    ) + bias[...]
    expo = jnp.exp(logit - jnp.max(logit, 1, keepdims=True))
    inverse = 1.0 / jnp.sum(expo, 1, keepdims=True)
    weights = expo.astype(BF16)

    def collect(lines_value, keep):
        kept = jnp.where(keep, lines_value * inverse, 0.0)
        return jnp.sum(kept.reshape(rows, PACK, WIDTH), 1)

    for i in range(rows):
        part = slice(i * PACK, (i + 1) * PACK)
        pair_part[part, :] = dot(weights[part], pair[i]) * inverse[part]
    node_part = collect(dot(weights, value), of_head)
    shifted = [collect(dot(weights, points[a]), of_value) - trans[a] for a in range(3)]
    local = [
        rotate[0][a] * shifted[0] + rotate[1][a] * shifted[1] + rotate[2][a] * shifted[2]
        for a in range(3)
    ]
    length = jnp.sqrt(
        local[0] * local[0] + local[1] * local[1] + local[2] * local[2] + point_eps
    )
    wide_part = jnp.concatenate(
        [pair_part[pl.ds(h, rows, stride=PACK), :] for h in range(HEADS)], 1
    ).astype(BF16)
    loads[4].wait()
    update = dot(node_part.astype(BF16), w_out[:WIDTH, :]) + b_out[...]
    for k, part in enumerate(local + [length]):
        update = update + dot(part.astype(BF16), w_local[k])
    update = update + dot(wide_part, w_out[WIDTH + 4 * HEADS * V_POINTS :, :])
    first = layer_norm(nodes.astype(F32) + update).astype(BF16)
    hidden = jnp.maximum(dot(first, w_trans[0]), 0.0).astype(BF16)
    hidden = jnp.maximum(dot(hidden, w_trans[1]), 0.0).astype(BF16)
    last = dot(hidden, w_trans[2])
    own_line = iota((rows, count), 1) == me * rows + iota((rows, count), 0)
    own_mask = jnp.sum(jnp.where(own_line, mask_ref[...], 0), 1, keepdims=True)
    result = (layer_norm(first.astype(F32) + last) * own_mask.astype(F32)).astype(BF16)
    own_end[...] = dot(result, w_edge_node[...]).astype(BF16)
    exchange(own_end, ends, send_b, recv_b)
    node_out[...] = result
    own_out[...] = own_end[...].astype(F32)
    ends[mine, :] = own_end[...]
    settle(own_end, ends, send_b, recv_b)
    ends_out[...] = ends[...]


def edge_kernel(
    step_rows,
    pair,
    ends,
    own,
    mask_ref,
    w_in,
    b_in,
    w_mid,
    b_mid,
    w_last,
    b_last,
    out,
    near,
    mask_cols,
    w_first,
):
    me = lax.axis_index("row")
    step = pl.program_id(0)
    count = ends.shape[0]
    rows = own.shape[0]
    c = C_PAIR

    @pl.when(step == 0)
    def _():
        near[...] = dot(own[...].astype(BF16), w_in[c : c + EDGE_NODE, :]) + b_in[...]
        eye = iota((count, count), 0) == iota((count, count), 1)
        line = jnp.sum(jnp.where(eye, mask_ref[...], 0), 1, keepdims=True).astype(F32)
        mask_cols[...] = jnp.broadcast_to(line, mask_cols.shape)
        w_first[:c, :] = w_in[:c, :]
        w_first[c:, :] = w_in[c + EDGE_NODE :, :]

    far = ends[...]
    for r in range(step_rows):
        i = step * step_rows + r
        row = pair[r]
        near_row = near[pl.ds(i, 1), :]
        own_row = own[pl.ds(i, 1), :]
        mask_row = mask_cols[pl.ds(me * rows + i, 1), :]
        pre = dot(jnp.concatenate([row, far], 1), w_first[...]) + near_row
        first = jnp.maximum(pre.astype(BF16), 0.0)
        second = jnp.maximum(dot(first, w_mid[...]) + b_mid[...], 0.0)
        resid = jnp.concatenate(
            [
                second[:, :c] + row.astype(F32),
                second[:, c : c + EDGE_NODE] + own_row,
                second[:, c + EDGE_NODE :] + far.astype(F32),
            ],
            1,
        ).astype(BF16)
        last = dot(resid, w_last[...]) + b_last[...]
        out[r] = (layer_norm(last) * (mask_row * mask_cols[...])).astype(BF16)


def body(
    n,
    node_feats,
    pair_feats,
    trans,
    frame_seed,
    residue_mask,
    chain_index,
    w_qkv,
    w_points,
    w_bias,
    head_weights,
    chain_bias,
    w_out,
    b_out,
    w_trans,
    w_edge_node,
    w_edge_in,
    b_edge_in,
    w_edge_mid,
    b_edge_mid,
    w_edge_out,
    b_edge_out,
):
    rows, d_node = node_feats.shape
    count = rows * n
    lines = rows * PACK
    pad = jnp.zeros((rows, FRAME - 6), BF16)
    packed = jnp.concatenate([node_feats, trans, frame_seed.astype(BF16), pad], 1)
    mask_line = residue_mask[None]
    vmem = pl.BlockSpec(memory_space=pltpu.VMEM)
    hbm = pl.BlockSpec(memory_space=pl.ANY)
    node_out, ends, own = pl.pallas_call(
        functools.partial(node_kernel, n),
        out_shape=(
            jax.ShapeDtypeStruct((rows, d_node), BF16),
            jax.ShapeDtypeStruct((count, EDGE_NODE), BF16),
            jax.ShapeDtypeStruct((rows, EDGE_NODE), F32),
        ),
        in_specs=[vmem] * 8 + [hbm] * 5,
        out_specs=(vmem, vmem, vmem),
        scratch_shapes=[
            pltpu.VMEM((count, d_node + FRAME), BF16),
            pltpu.VMEM((count, EDGE_NODE), BF16),
            pltpu.VMEM((rows, EDGE_NODE), BF16),
            pltpu.VMEM(pair_feats.shape, BF16),
            pltpu.VMEM(w_qkv.shape, BF16),
            pltpu.VMEM(w_points.shape, BF16),
            pltpu.VMEM(w_out.shape, BF16),
            pltpu.VMEM(w_trans.shape, BF16),
            pltpu.VMEM((lines, count), F32),
            pltpu.VMEM((C_PAIR, 128), F32),
            pltpu.VMEM((4, WIDTH, d_node), BF16),
            pltpu.VMEM((lines, C_PAIR), F32),
            pltpu.SemaphoreType.DMA((5,)),
            pltpu.SemaphoreType.DMA((n,)),
            pltpu.SemaphoreType.DMA((n,)),
            pltpu.SemaphoreType.DMA((n,)),
            pltpu.SemaphoreType.DMA((n,)),
        ],
        compiler_params=pltpu.CompilerParams(
            collective_id=0, has_side_effects=True, vmem_limit_bytes=VMEM_LIMIT
        ),
        name="node",
    )(
        packed,
        mask_line,
        chain_index[None],
        w_bias,
        head_weights[None],
        chain_bias[None],
        b_out[None],
        w_edge_node,
        pair_feats,
        w_qkv,
        w_points,
        w_out,
        w_trans,
    )
    step_rows = 2 if count <= 512 else 1

    def fixed(array):
        return pl.BlockSpec(array.shape, lambda s: (0,) * array.ndim)

    constants = (
        ends,
        own,
        mask_line,
        w_edge_in,
        b_edge_in[None],
        w_edge_mid,
        b_edge_mid[None],
        w_edge_out,
        b_edge_out[None],
    )
    block = pl.BlockSpec((step_rows, count, C_PAIR), lambda s: (s, 0, 0))
    pair_out = pl.pallas_call(
        functools.partial(edge_kernel, step_rows),
        out_shape=jax.ShapeDtypeStruct(pair_feats.shape, BF16),
        grid=(rows // step_rows,),
        in_specs=[block] + [fixed(array) for array in constants],
        out_specs=block,
        scratch_shapes=[
            pltpu.VMEM((rows, w_edge_in.shape[1]), F32),
            pltpu.VMEM((count, C_PAIR), F32),
            pltpu.VMEM((C_PAIR + EDGE_NODE, w_edge_in.shape[1]), BF16),
        ],
        compiler_params=pltpu.CompilerParams(vmem_limit_bytes=VMEM_LIMIT),
        name="edge",
    )(pair_feats, *constants)
    return (node_out, pair_out)


def solution(mesh):
    split = P(("grp", "row"), None)
    in_specs = (
        split,
        P(("grp", "row"), None, None),
        split,
        split,
        P("grp"),
        P("grp"),
    ) + (P(),) * 15
    out_specs = (split, P(("grp", "row"), None, None))
    return jax.shard_map(
        functools.partial(body, mesh.shape["row"]),
        mesh=mesh,
        in_specs=in_specs,
        out_specs=out_specs,
        check_vma=False,
    )
```

```python
import functools
import math

import jax
import jax.numpy as jnp
from jax import lax
from jax.experimental import pallas as pl
from jax.experimental.pallas import tpu as pltpu
from jax.sharding import PartitionSpec as P

C_PAIR = 128
HEADS = 12
HEAD_DIM = 16
QK_POINTS = 4
V_POINTS = 8
POINTS = 2 * QK_POINTS + V_POINTS
EDGE_NODE = 128
WIDTH = HEADS * HEAD_DIM
PACK = 16
FRAME = 128

mask_bias = 100000.0
norm_eps = 1e-05
point_eps = 1e-08
F32 = jnp.float32
BF16 = jnp.bfloat16
MESH = pl.DeviceIdType.MESH
VMEM_LIMIT = 60 << 20


def dot(a, b):
    return jnp.dot(a, b, preferred_element_type=F32)


def dot_nt(a, b):
    return lax.dot_general(a, b, (((1,), (1,)), ((), ())), preferred_element_type=F32)


def layer_norm(values):
    centred = values - jnp.mean(values, -1, keepdims=True)
    return centred * lax.rsqrt(jnp.mean(centred * centred, -1, keepdims=True) + norm_eps)


def cos_sin(steps):
    quarter = jnp.floor((steps + 32.0) * (1.0 / 64.0))
    x = (steps - 64.0 * quarter) * (2.0 * math.pi / 256.0)
    y = x * x
    c = 1.0 + y * (-0.5 + y * (1 / 24 + y * (-1 / 720 + y * (1 / 40320 - y * (1 / 3628800)))))
    s = x * (1.0 + y * (-1 / 6 + y * (1 / 120 + y * (-1 / 5040 + y * (1 / 362880)))))
    one, two, three = quarter == 1.0, quarter == 2.0, quarter == 3.0
    cosine = jnp.where(one, -s, jnp.where(two, -c, jnp.where(three, s, c)))
    sine = jnp.where(one, c, jnp.where(two, -s, jnp.where(three, -c, s)))
    return cosine, sine


def frames(frame):
    cosine, sine = cos_sin(frame)
    c0, c1, c2 = (cosine[:, k : k + 1] for k in (3, 4, 5))
    s0, s1, s2 = (sine[:, k : k + 1] for k in (3, 4, 5))
    rotate = (
        (c0 * c1 * c2 - s0 * s2, -c0 * c1 * s2 - s0 * c2, c0 * s1),
        (s0 * c1 * c2 + c0 * s2, c0 * c2 - s0 * c1 * s2, s0 * s1),
        (-s1 * c2, s1 * s2, c1),
    )
    return rotate, tuple(frame[:, k : k + 1] for k in range(3))


def spatial_points(nodes, rotate, trans, w_points):
    local = [dot_nt(nodes, w_points[b * WIDTH : (b + 1) * WIDTH, :]) for b in range(3)]
    return [
        (
            rotate[a][0] * local[0] + rotate[a][1] * local[1] + rotate[a][2] * local[2] + trans[a]
        ).astype(BF16)
        for a in range(3)
    ]


def iota(shape, axis):
    return lax.broadcasted_iota(jnp.int32, shape, axis)


def node_kernel(
    n,
    node_feats,
    trans_ref,
    seed_ref,
    mask_ref,
    chain_ref,
    w_bias,
    head_weights,
    chain_bias,
    b_out,
    w_edge_node,
    pair_hbm,
    w_qkv_hbm,
    w_points_hbm,
    w_out_hbm,
    w_trans_hbm,
    node_out,
    ends_out,
    own_out,
    packed,
    gathered,
    ends,
    own_end,
    pair,
    w_qkv,
    w_points,
    w_out,
    w_trans,
    bias,
    wide,
    w_local,
    pair_part,
    load_sem,
    send_a,
    recv_a,
    send_b,
    recv_b,
):
    me = lax.axis_index("row")
    rows = packed.shape[0]
    count = rows * n
    lines = rows * PACK

    barrier = pltpu.get_barrier_semaphore()

    def greet(s, carry):
        pl.semaphore_signal(
            barrier, inc=1, device_id={"row": lax.rem(me + s, n)}, device_id_type=MESH
        )
        return carry

    lax.fori_loop(1, n, greet, 0)
    loads = [
        pltpu.make_async_copy(src, dst, load_sem.at[k])
        for k, (src, dst) in enumerate(
            (
                (pair_hbm, pair),
                (w_qkv_hbm, w_qkv),
                (w_points_hbm, w_points),
                (w_out_hbm, w_out),
                (w_trans_hbm, w_trans),
            )
        )
    ]
    for load in loads:
        load.start()
    wide[...] = jnp.zeros_like(wide)
    wide[:3, :rows] = trans_ref[...].astype(F32)
    wide[3:6, :rows] = seed_ref[...].astype(F32)
    packed[:, :-FRAME] = node_feats[...]
    packed[:, -FRAME:] = wide[...].T[:rows].astype(BF16)
    wide[:HEADS, :] = w_bias[...].astype(F32)
    wide[HEADS:PACK, :] = jnp.zeros((PACK - HEADS, C_PAIR), F32)
    w_bias_t = wide[:PACK, :].astype(BF16)
    pl.semaphore_wait(barrier, n - 1)

    def copy_of(s, src, dst, send, recv):
        return pltpu.make_async_remote_copy(
            src_ref=src,
            dst_ref=dst.at[pl.ds(pl.multiple_of(me * rows, rows), rows)],
            send_sem=send.at[s],
            recv_sem=recv.at[s],
            device_id={"row": lax.rem(me + s, n)},
            device_id_type=MESH,
        )

    def exchange(src, dst, send, recv):
        def go(s, carry):
            copy_of(s, src, dst, send, recv).start()
            return carry

        lax.fori_loop(1, n, go, 0)

    def settle(src, dst, send, recv):
        def go(s, carry):
            copy_of(s, src, dst, send, recv).wait()
            return carry

        lax.fori_loop(1, n, go, 0)

    exchange(packed, gathered, send_a, recv_a)
    mine = pl.ds(pl.multiple_of(me * rows, rows), rows)
    gathered[mine, :] = packed[...]

    loads[0].wait()

    def bias_row(i, carry):
        bias[pl.ds(pl.multiple_of(i * PACK, PACK), PACK), :] = dot_nt(w_bias_t, pair[i])
        return carry

    lax.fori_loop(0, rows, bias_row, 0, unroll=4)

    line = iota((lines, 1), 0)
    line_head = line % PACK
    line_row = line // PACK
    at_own = iota((lines, count), 1) == me * rows + line_row
    chain_q = jnp.sum(jnp.where(at_own, chain_ref[...], 0), 1, keepdims=True)
    mask_q = jnp.sum(jnp.where(at_own, mask_ref[...], 0), 1, keepdims=True)
    at_head = iota((lines, HEADS), 1) == line_head
    gamma = jnp.sum(jnp.where(at_head, jax.nn.softplus(head_weights[...]), 0.0), 1, keepdims=True)
    chain_add = jnp.sum(jnp.where(at_head, chain_bias[...], 0.0), 1, keepdims=True)
    column = iota((lines, WIDTH), 1)
    of_head = column // HEAD_DIM == line_head
    of_key = of_head & (column % POINTS >= QK_POINTS) & (column % POINTS < 2 * QK_POINTS)
    of_value = of_head & (column % POINTS >= 2 * QK_POINTS)
    spread = (iota((lines, rows), 1) == line_row).astype(BF16)
    same = (chain_q == chain_ref[...]).astype(F32)
    pair_mask = (mask_q * mask_ref[...]).astype(F32)
    bias[...] = bias[...] * math.sqrt(1.0 / 3.0) + (
        chain_add * same + mask_bias * (pair_mask - 1.0)
    )

    loads[1].wait()
    loads[2].wait()
    nodes = packed[:, :-FRAME]
    rotate, trans = frames(packed[:, -FRAME:].astype(F32))
    query = dot_nt(nodes, w_qkv[:WIDTH, :]).astype(BF16)
    own_points = spatial_points(nodes, rotate, trans, w_points)
    q_lines = jnp.where(of_head, dot(spread, query), 0.0).astype(BF16)
    p_lines = [
        jnp.where(of_key, pltpu.roll(dot(spread, own_points[a]), QK_POINTS, 1), 0.0)
        for a in range(3)
    ]
    q_square = sum(jnp.sum(p * p, 1, keepdims=True) for p in p_lines)
    p_lines = [(-2.0 * p).astype(BF16) for p in p_lines]
    ones_key = of_key.astype(BF16)

    loads[3].wait()
    for k in range(4):
        start = WIDTH + k * HEADS * V_POINTS
        block = w_out[start : start + HEADS * V_POINTS, :].astype(F32)
        block = block.reshape(HEADS, V_POINTS, -1)
        block = jnp.concatenate([jnp.zeros_like(block), block], 1)
        w_local[k] = block.reshape(WIDTH, -1).astype(BF16)

    settle(packed, gathered, send_a, recv_a)

    every = gathered[:, :-FRAME]
    key = dot_nt(every, w_qkv[WIDTH : 2 * WIDTH, :]).astype(BF16)
    value = dot_nt(every, w_qkv[2 * WIDTH :, :]).astype(BF16)
    rotate_all, trans_all = frames(gathered[:, -FRAME:].astype(F32))
    points = spatial_points(every, rotate_all, trans_all, w_points)
    square = sum(p.astype(F32) * p.astype(F32) for p in points)
    high = square.astype(BF16)
    rest = square - high.astype(F32)
    middle = rest.astype(BF16)
    low = (rest - middle.astype(F32)).astype(BF16)
    dots = dot_nt(q_lines, key)
    distance = q_square + (
        dot_nt(p_lines[0], points[0])
        + dot_nt(p_lines[1], points[1])
        + dot_nt(p_lines[2], points[2])
        + dot_nt(ones_key, high)
        + dot_nt(ones_key, middle)
        + dot_nt(ones_key, low)
    )
    weight_c = math.sqrt(2.0 / (9.0 * QK_POINTS))
    third = math.sqrt(1.0 / 3.0)
    logit = (
        dots * (third / math.sqrt(HEAD_DIM)) - (0.5 * weight_c * third) * gamma * distance
    ) + bias[...]
    expo = jnp.exp(logit - jnp.max(logit, 1, keepdims=True))
    inverse = 1.0 / jnp.sum(expo, 1, keepdims=True)
    weights = expo.astype(BF16)

    def collect(lines_value, keep):
        kept = jnp.where(keep, lines_value * inverse, 0.0)
        return jnp.sum(kept.reshape(rows, PACK, WIDTH), 1)

    for i in range(rows):
        part = slice(i * PACK, (i + 1) * PACK)
        pair_part[part, :] = dot(weights[part], pair[i]) * inverse[part]
    node_part = collect(dot(weights, value), of_head)
    shifted = [collect(dot(weights, points[a]), of_value) - trans[a] for a in range(3)]
    local = [
        rotate[0][a] * shifted[0] + rotate[1][a] * shifted[1] + rotate[2][a] * shifted[2]
        for a in range(3)
    ]
    length = jnp.sqrt(
        local[0] * local[0] + local[1] * local[1] + local[2] * local[2] + point_eps
    )
    wide_part = jnp.concatenate(
        [pair_part[pl.ds(h, rows, stride=PACK), :] for h in range(HEADS)], 1
    ).astype(BF16)
    loads[4].wait()
    update = dot(node_part.astype(BF16), w_out[:WIDTH, :]) + b_out[...]
    for k, part in enumerate(local + [length]):
        update = update + dot(part.astype(BF16), w_local[k])
    update = update + dot(wide_part, w_out[WIDTH + 4 * HEADS * V_POINTS :, :])
    first = layer_norm(nodes.astype(F32) + update).astype(BF16)
    hidden = jnp.maximum(dot(first, w_trans[0]), 0.0).astype(BF16)
    hidden = jnp.maximum(dot(hidden, w_trans[1]), 0.0).astype(BF16)
    last = dot(hidden, w_trans[2])
    own_line = iota((rows, count), 1) == me * rows + iota((rows, count), 0)
    own_mask = jnp.sum(jnp.where(own_line, mask_ref[...], 0), 1, keepdims=True)
    result = (layer_norm(first.astype(F32) + last) * own_mask.astype(F32)).astype(BF16)
    own_end[...] = dot(result, w_edge_node[...]).astype(BF16)
    exchange(own_end, ends, send_b, recv_b)
    node_out[...] = result
    own_out[...] = own_end[...].astype(F32)
    ends[mine, :] = own_end[...]
    settle(own_end, ends, send_b, recv_b)
    ends_out[...] = ends[...]


def edge_kernel(
    step_rows,
    pair,
    ends,
    own,
    nodes,
    mask_ref,
    w_in,
    b_in,
    w_mid,
    b_mid,
    w_last,
    b_last,
    node_out,
    out,
    near,
    mask_cols,
    w_first,
):
    me = lax.axis_index("row")
    step = pl.program_id(0)
    count = ends.shape[0]
    rows = own.shape[0]
    c = C_PAIR

    @pl.when(step == 0)
    def _():
        near[...] = dot(own[...].astype(BF16), w_in[c : c + EDGE_NODE, :]) + b_in[...][None, :]
        node_out[...] = nodes[...]
        eye = iota((count, count), 0) == iota((count, count), 1)
        line = jnp.sum(jnp.where(eye, mask_ref[...], 0), 1, keepdims=True).astype(F32)
        mask_cols[...] = jnp.broadcast_to(line, mask_cols.shape)
        w_first[:c, :] = w_in[:c, :]
        w_first[c:, :] = w_in[c + EDGE_NODE :, :]

    far = ends[...]
    for r in range(step_rows):
        i = step * step_rows + r
        row = pair[r]
        near_row = near[pl.ds(i, 1), :]
        own_row = own[pl.ds(i, 1), :]
        mask_row = mask_cols[pl.ds(me * rows + i, 1), :]
        pre = dot(jnp.concatenate([row, far], 1), w_first[...]) + near_row
        first = jnp.maximum(pre.astype(BF16), 0.0)
        second = jnp.maximum(dot(first, w_mid[...]) + b_mid[...][None, :], 0.0)
        resid = jnp.concatenate(
            [
                second[:, :c] + row.astype(F32),
                second[:, c : c + EDGE_NODE] + own_row,
                second[:, c + EDGE_NODE :] + far.astype(F32),
            ],
            1,
        ).astype(BF16)
        last = dot(resid, w_last[...]) + b_last[...]
        out[r] = (layer_norm(last) * (mask_row * mask_cols[...])).astype(BF16)


def body(
    n,
    node_feats,
    pair_feats,
    trans,
    frame_seed,
    residue_mask,
    chain_index,
    w_qkv,
    w_points,
    w_bias,
    head_weights,
    chain_bias,
    w_out,
    b_out,
    w_trans,
    w_edge_node,
    w_edge_in,
    b_edge_in,
    w_edge_mid,
    b_edge_mid,
    w_edge_out,
    b_edge_out,
):
    rows, d_node = node_feats.shape
    count = rows * n
    lines = rows * PACK
    mask_line = residue_mask[None]
    vmem = pl.BlockSpec(memory_space=pltpu.VMEM)
    hbm = pl.BlockSpec(memory_space=pl.ANY)
    nodes, ends, own = pl.pallas_call(
        functools.partial(node_kernel, n),
        out_shape=(
            jax.ShapeDtypeStruct((rows, d_node), BF16),
            jax.ShapeDtypeStruct((count, EDGE_NODE), BF16),
            jax.ShapeDtypeStruct((rows, EDGE_NODE), F32),
        ),
        in_specs=[vmem] * 10 + [hbm] * 5,
        out_specs=(vmem, vmem, vmem),
        scratch_shapes=[
            pltpu.VMEM((rows, d_node + FRAME), BF16),
            pltpu.VMEM((count, d_node + FRAME), BF16),
            pltpu.VMEM((count, EDGE_NODE), BF16),
            pltpu.VMEM((rows, EDGE_NODE), BF16),
            pltpu.VMEM(pair_feats.shape, BF16),
            pltpu.VMEM(w_qkv.shape[::-1], BF16),
            pltpu.VMEM(w_points.shape[::-1], BF16),
            pltpu.VMEM(w_out.shape, BF16),
            pltpu.VMEM(w_trans.shape, BF16),
            pltpu.VMEM((lines, count), F32),
            pltpu.VMEM((FRAME, FRAME), F32),
            pltpu.VMEM((4, WIDTH, d_node), BF16),
            pltpu.VMEM((lines, C_PAIR), F32),
            pltpu.SemaphoreType.DMA((5,)),
            pltpu.SemaphoreType.DMA((n,)),
            pltpu.SemaphoreType.DMA((n,)),
            pltpu.SemaphoreType.DMA((n,)),
            pltpu.SemaphoreType.DMA((n,)),
        ],
        compiler_params=pltpu.CompilerParams(
            collective_id=0, has_side_effects=True, vmem_limit_bytes=VMEM_LIMIT
        ),
        name="node",
    )(
        node_feats,
        trans.T,
        frame_seed.T,
        mask_line,
        chain_index[None],
        w_bias.T,
        head_weights[None],
        chain_bias[None],
        b_out[None],
        w_edge_node,
        pair_feats,
        w_qkv.T,
        w_points.T,
        w_out,
        w_trans,
    )
    step_rows = 2 if count <= 512 else 1

    def fixed(array):
        return pl.BlockSpec(array.shape, lambda s: (0,) * array.ndim)

    constants = (
        ends,
        own,
        nodes,
        mask_line,
        w_edge_in,
        b_edge_in,
        w_edge_mid,
        b_edge_mid,
        w_edge_out,
        b_edge_out[None],
    )
    block = pl.BlockSpec((step_rows, count, C_PAIR), lambda s: (s, 0, 0))
    return pl.pallas_call(
        functools.partial(edge_kernel, step_rows),
        out_shape=(
            jax.ShapeDtypeStruct((rows, d_node), BF16),
            jax.ShapeDtypeStruct(pair_feats.shape, BF16),
        ),
        grid=(rows // step_rows,),
        in_specs=[block] + [fixed(array) for array in constants],
        out_specs=(fixed(nodes), block),
        scratch_shapes=[
            pltpu.VMEM((rows, w_edge_in.shape[1]), F32),
            pltpu.VMEM((count, C_PAIR), F32),
            pltpu.VMEM((C_PAIR + EDGE_NODE, w_edge_in.shape[1]), BF16),
        ],
        compiler_params=pltpu.CompilerParams(vmem_limit_bytes=VMEM_LIMIT),
        name="edge",
    )(pair_feats, *constants)


def solution(mesh):
    split = P(("grp", "row"), None)
    in_specs = (
        split,
        P(("grp", "row"), None, None),
        split,
        split,
        P("grp"),
        P("grp"),
    ) + (P(),) * 15
    out_specs = (split, P(("grp", "row"), None, None))
    return jax.shard_map(
        functools.partial(body, mesh.shape["row"]),
        mesh=mesh,
        in_specs=in_specs,
        out_specs=out_specs,
        check_vma=False,
    )
```

```python
import functools
import math

import jax
import jax.numpy as jnp
from jax import lax
from jax.experimental import pallas as pl
from jax.experimental.pallas import tpu as pltpu
from jax.sharding import PartitionSpec as P

C_PAIR = 128
HEADS = 12
HEAD_DIM = 16
QK_POINTS = 4
V_POINTS = 8
POINTS = 2 * QK_POINTS + V_POINTS
EDGE_NODE = 128
WIDTH = HEADS * HEAD_DIM
PACK = 16
FRAME = 128

mask_bias = 100000.0
norm_eps = 1e-05
point_eps = 1e-08
F32 = jnp.float32
BF16 = jnp.bfloat16
MESH = pl.DeviceIdType.MESH
VMEM_LIMIT = 60 << 20


def dot(a, b):
    return jnp.dot(a, b, preferred_element_type=F32)


def dot_nt(a, b):
    return lax.dot_general(a, b, (((1,), (1,)), ((), ())), preferred_element_type=F32)


def layer_norm(values):
    centred = values - jnp.mean(values, -1, keepdims=True)
    return centred * lax.rsqrt(jnp.mean(centred * centred, -1, keepdims=True) + norm_eps)


def cos_sin(steps):
    quarter = jnp.floor((steps + 32.0) * (1.0 / 64.0))
    x = (steps - 64.0 * quarter) * (2.0 * math.pi / 256.0)
    y = x * x
    c = 1.0 + y * (-0.5 + y * (1 / 24 + y * (-1 / 720 + y * (1 / 40320 - y * (1 / 3628800)))))
    s = x * (1.0 + y * (-1 / 6 + y * (1 / 120 + y * (-1 / 5040 + y * (1 / 362880)))))
    one, two, three = quarter == 1.0, quarter == 2.0, quarter == 3.0
    cosine = jnp.where(one, -s, jnp.where(two, -c, jnp.where(three, s, c)))
    sine = jnp.where(one, c, jnp.where(two, -s, jnp.where(three, -c, s)))
    return cosine, sine


def frames(frame):
    cosine, sine = cos_sin(frame)
    c0, c1, c2 = (cosine[:, k : k + 1] for k in (3, 4, 5))
    s0, s1, s2 = (sine[:, k : k + 1] for k in (3, 4, 5))
    rotate = (
        (c0 * c1 * c2 - s0 * s2, -c0 * c1 * s2 - s0 * c2, c0 * s1),
        (s0 * c1 * c2 + c0 * s2, c0 * c2 - s0 * c1 * s2, s0 * s1),
        (-s1 * c2, s1 * s2, c1),
    )
    return rotate, tuple(frame[:, k : k + 1] for k in range(3))


def spatial_points(nodes, rotate, trans, w_points):
    local = [dot_nt(nodes, w_points[b * WIDTH : (b + 1) * WIDTH, :]) for b in range(3)]
    return [
        (
            rotate[a][0] * local[0] + rotate[a][1] * local[1] + rotate[a][2] * local[2] + trans[a]
        ).astype(BF16)
        for a in range(3)
    ]


def iota(shape, axis):
    return lax.broadcasted_iota(jnp.int32, shape, axis)


def node_kernel(
    n,
    node_feats,
    trans_ref,
    seed_ref,
    mask_ref,
    chain_ref,
    w_bias,
    head_weights,
    chain_bias,
    b_out,
    w_edge_node,
    pair_hbm,
    w_qkv_hbm,
    w_points_hbm,
    w_out_hbm,
    w_trans_hbm,
    w_in_hbm,
    node_out,
    ends_out,
    own_out,
    pre_hbm,
    packed,
    gathered,
    ends,
    own_end,
    pair,
    w_qkv,
    w_points,
    w_out,
    w_trans,
    w_in,
    pre,
    bias,
    wide,
    w_local,
    pair_part,
    load_sem,
    send_a,
    recv_a,
    send_b,
    recv_b,
):
    me = lax.axis_index("row")
    rows = packed.shape[0]
    count = rows * n
    lines = rows * PACK

    barrier = pltpu.get_barrier_semaphore()

    def greet(s, carry):
        pl.semaphore_signal(
            barrier, inc=1, device_id={"row": lax.rem(me + s, n)}, device_id_type=MESH
        )
        return carry

    lax.fori_loop(1, n, greet, 0)
    loads = [
        pltpu.make_async_copy(src, dst, load_sem.at[k])
        for k, (src, dst) in enumerate(
            (
                (pair_hbm, pair),
                (w_qkv_hbm, w_qkv),
                (w_points_hbm, w_points),
                (w_out_hbm, w_out),
                (w_trans_hbm, w_trans),
                (w_in_hbm.at[pl.ds(0, C_PAIR)], w_in),
            )
        )
    ]
    for load in loads:
        load.start()
    wide[...] = jnp.zeros_like(wide)
    wide[:3, :rows] = trans_ref[...].astype(F32)
    wide[3:6, :rows] = seed_ref[...].astype(F32)
    packed[:, :-FRAME] = node_feats[...]
    packed[:, -FRAME:] = wide[...].T[:rows].astype(BF16)
    wide[:HEADS, :] = w_bias[...].astype(F32)
    wide[HEADS:PACK, :] = jnp.zeros((PACK - HEADS, C_PAIR), F32)
    w_bias_t = wide[:PACK, :].astype(BF16)

    def copy_of(s, src, dst, send, recv):
        return pltpu.make_async_remote_copy(
            src_ref=src,
            dst_ref=dst.at[pl.ds(pl.multiple_of(me * rows, rows), rows)],
            send_sem=send.at[s],
            recv_sem=recv.at[s],
            device_id={"row": lax.rem(me + s, n)},
            device_id_type=MESH,
        )

    def exchange(src, dst, send, recv):
        def go(s, carry):
            copy_of(s, src, dst, send, recv).start()
            return carry

        lax.fori_loop(1, n, go, 0)

    def settle(src, dst, send, recv):
        def go(s, carry):
            copy_of(s, src, dst, send, recv).wait()
            return carry

        lax.fori_loop(1, n, go, 0)

    mine = pl.ds(pl.multiple_of(me * rows, rows), rows)
    gathered[mine, :] = packed[...]

    loads[0].wait()

    def bias_row(i, carry):
        bias[pl.ds(pl.multiple_of(i * PACK, PACK), PACK), :] = dot_nt(w_bias_t, pair[i])
        return carry

    lax.fori_loop(0, rows, bias_row, 0, unroll=4)

    line = iota((lines, 1), 0)
    line_head = line % PACK
    line_row = line // PACK
    at_own = iota((lines, count), 1) == me * rows + line_row
    chain_q = jnp.sum(jnp.where(at_own, chain_ref[...], 0), 1, keepdims=True)
    mask_q = jnp.sum(jnp.where(at_own, mask_ref[...], 0), 1, keepdims=True)
    at_head = iota((lines, HEADS), 1) == line_head
    gamma = jnp.sum(jnp.where(at_head, jax.nn.softplus(head_weights[...]), 0.0), 1, keepdims=True)
    chain_add = jnp.sum(jnp.where(at_head, chain_bias[...], 0.0), 1, keepdims=True)
    column = iota((lines, WIDTH), 1)
    of_head = column // HEAD_DIM == line_head
    of_key = of_head & (column % POINTS >= QK_POINTS) & (column % POINTS < 2 * QK_POINTS)
    of_value = of_head & (column % POINTS >= 2 * QK_POINTS)
    spread = (iota((lines, rows), 1) == line_row).astype(BF16)
    same = (chain_q == chain_ref[...]).astype(F32)
    pair_mask = (mask_q * mask_ref[...]).astype(F32)
    bias[...] = bias[...] * math.sqrt(1.0 / 3.0) + (
        chain_add * same + mask_bias * (pair_mask - 1.0)
    )

    loads[1].wait()
    loads[2].wait()
    nodes = packed[:, :-FRAME]
    rotate, trans = frames(packed[:, -FRAME:].astype(F32))
    query = dot_nt(nodes, w_qkv[:WIDTH, :]).astype(BF16)
    own_points = spatial_points(nodes, rotate, trans, w_points)
    q_lines = jnp.where(of_head, dot(spread, query), 0.0).astype(BF16)
    p_lines = [
        jnp.where(of_key, pltpu.roll(dot(spread, own_points[a]), QK_POINTS, 1), 0.0)
        for a in range(3)
    ]
    q_square = sum(jnp.sum(p * p, 1, keepdims=True) for p in p_lines)
    p_lines = [(-2.0 * p).astype(BF16) for p in p_lines]
    ones_key = of_key.astype(BF16)

    loads[3].wait()
    for k in range(4):
        start = WIDTH + k * HEADS * V_POINTS
        block = w_out[start : start + HEADS * V_POINTS, :].astype(F32)
        block = block.reshape(HEADS, V_POINTS, -1)
        block = jnp.concatenate([jnp.zeros_like(block), block], 1)
        w_local[k] = block.reshape(WIDTH, -1).astype(BF16)

    pl.semaphore_wait(barrier, n - 1)
    exchange(packed, gathered, send_a, recv_a)
    loads[5].wait()

    def pair_row(i, carry):
        pre[i] = dot(pair[i], w_in[...]).astype(BF16)
        return carry

    lax.fori_loop(0, rows, pair_row, 0, unroll=2)
    put_pre = pltpu.make_async_copy(pre, pre_hbm, load_sem.at[6])
    put_pre.start()
    settle(packed, gathered, send_a, recv_a)

    every = gathered[:, :-FRAME]
    key = dot_nt(every, w_qkv[WIDTH : 2 * WIDTH, :]).astype(BF16)
    value = dot_nt(every, w_qkv[2 * WIDTH :, :]).astype(BF16)
    rotate_all, trans_all = frames(gathered[:, -FRAME:].astype(F32))
    points = spatial_points(every, rotate_all, trans_all, w_points)
    square = sum(p.astype(F32) * p.astype(F32) for p in points)
    high = square.astype(BF16)
    rest = square - high.astype(F32)
    middle = rest.astype(BF16)
    low = (rest - middle.astype(F32)).astype(BF16)
    dots = dot_nt(q_lines, key)
    distance = q_square + (
        dot_nt(p_lines[0], points[0])
        + dot_nt(p_lines[1], points[1])
        + dot_nt(p_lines[2], points[2])
        + dot_nt(ones_key, high)
        + dot_nt(ones_key, middle)
        + dot_nt(ones_key, low)
    )
    weight_c = math.sqrt(2.0 / (9.0 * QK_POINTS))
    third = math.sqrt(1.0 / 3.0)
    logit = (
        dots * (third / math.sqrt(HEAD_DIM)) - (0.5 * weight_c * third) * gamma * distance
    ) + bias[...]
    expo = jnp.exp(logit - jnp.max(logit, 1, keepdims=True))
    inverse = 1.0 / jnp.sum(expo, 1, keepdims=True)
    weights = expo.astype(BF16)

    def collect(lines_value, keep):
        kept = jnp.where(keep, lines_value * inverse, 0.0)
        return jnp.sum(kept.reshape(rows, PACK, WIDTH), 1)

    for i in range(rows):
        part = slice(i * PACK, (i + 1) * PACK)
        pair_part[part, :] = dot(weights[part], pair[i]) * inverse[part]
    node_part = collect(dot(weights, value), of_head)
    shifted = [collect(dot(weights, points[a]), of_value) - trans[a] for a in range(3)]
    local = [
        rotate[0][a] * shifted[0] + rotate[1][a] * shifted[1] + rotate[2][a] * shifted[2]
        for a in range(3)
    ]
    length = jnp.sqrt(
        local[0] * local[0] + local[1] * local[1] + local[2] * local[2] + point_eps
    )
    wide_part = jnp.concatenate(
        [pair_part[pl.ds(h, rows, stride=PACK), :] for h in range(HEADS)], 1
    ).astype(BF16)
    loads[4].wait()
    update = dot(node_part.astype(BF16), w_out[:WIDTH, :]) + b_out[...]
    for k, part in enumerate(local + [length]):
        update = update + dot(part.astype(BF16), w_local[k])
    update = update + dot(wide_part, w_out[WIDTH + 4 * HEADS * V_POINTS :, :])
    first = layer_norm(nodes.astype(F32) + update).astype(BF16)
    hidden = jnp.maximum(dot(first, w_trans[0]), 0.0).astype(BF16)
    hidden = jnp.maximum(dot(hidden, w_trans[1]), 0.0).astype(BF16)
    last = dot(hidden, w_trans[2])
    own_line = iota((rows, count), 1) == me * rows + iota((rows, count), 0)
    own_mask = jnp.sum(jnp.where(own_line, mask_ref[...], 0), 1, keepdims=True)
    result = (layer_norm(first.astype(F32) + last) * own_mask.astype(F32)).astype(BF16)
    own_end[...] = dot(result, w_edge_node[...]).astype(BF16)
    exchange(own_end, ends, send_b, recv_b)
    node_out[...] = result
    own_out[...] = own_end[...].astype(F32)
    ends[mine, :] = own_end[...]
    settle(own_end, ends, send_b, recv_b)
    ends_out[...] = ends[...]
    put_pre.wait()


def edge_kernel(
    step_rows,
    pair,
    pre0,
    ends,
    own,
    nodes,
    mask_ref,
    w_in,
    b_in,
    w_mid,
    b_mid,
    w_last,
    b_last,
    node_out,
    out,
    near,
    mask_cols,
    far_in,
):
    me = lax.axis_index("row")
    step = pl.program_id(0)
    count = ends.shape[0]
    rows = own.shape[0]
    c = C_PAIR

    @pl.when(step == 0)
    def _():
        near[...] = dot(own[...].astype(BF16), w_in[c : c + EDGE_NODE, :]) + b_in[...][None, :]
        node_out[...] = nodes[...]
        eye = iota((count, count), 0) == iota((count, count), 1)
        line = jnp.sum(jnp.where(eye, mask_ref[...], 0), 1, keepdims=True).astype(F32)
        mask_cols[...] = jnp.broadcast_to(line, mask_cols.shape)
        far_in[...] = dot(ends[...], w_in[c + EDGE_NODE :, :])

    far = ends[...]
    for r in range(step_rows):
        i = step * step_rows + r
        row = pair[r]
        near_row = near[pl.ds(i, 1), :]
        own_row = own[pl.ds(i, 1), :]
        mask_row = mask_cols[pl.ds(me * rows + i, 1), :]
        pre = pre0[r].astype(F32) + (far_in[...] + near_row)
        first = jnp.maximum(pre.astype(BF16), 0.0)
        second = jnp.maximum(dot(first, w_mid[...]) + b_mid[...][None, :], 0.0)
        resid = jnp.concatenate(
            [
                second[:, :c] + row.astype(F32),
                second[:, c : c + EDGE_NODE] + own_row,
                second[:, c + EDGE_NODE :] + far.astype(F32),
            ],
            1,
        ).astype(BF16)
        last = dot(resid, w_last[...]) + b_last[...]
        out[r] = (layer_norm(last) * (mask_row * mask_cols[...])).astype(BF16)


def body(
    n,
    node_feats,
    pair_feats,
    trans,
    frame_seed,
    residue_mask,
    chain_index,
    w_qkv,
    w_points,
    w_bias,
    head_weights,
    chain_bias,
    w_out,
    b_out,
    w_trans,
    w_edge_node,
    w_edge_in,
    b_edge_in,
    w_edge_mid,
    b_edge_mid,
    w_edge_out,
    b_edge_out,
):
    rows, d_node = node_feats.shape
    count = rows * n
    lines = rows * PACK
    mask_line = residue_mask[None]
    vmem = pl.BlockSpec(memory_space=pltpu.VMEM)
    hbm = pl.BlockSpec(memory_space=pl.ANY)
    nodes, ends, own, pre = pl.pallas_call(
        functools.partial(node_kernel, n),
        out_shape=(
            jax.ShapeDtypeStruct((rows, d_node), BF16),
            jax.ShapeDtypeStruct((count, EDGE_NODE), BF16),
            jax.ShapeDtypeStruct((rows, EDGE_NODE), F32),
            jax.ShapeDtypeStruct((rows, count, w_edge_in.shape[1]), BF16),
        ),
        in_specs=[vmem] * 10 + [hbm] * 6,
        out_specs=(vmem, vmem, vmem, hbm),
        scratch_shapes=[
            pltpu.VMEM((rows, d_node + FRAME), BF16),
            pltpu.VMEM((count, d_node + FRAME), BF16),
            pltpu.VMEM((count, EDGE_NODE), BF16),
            pltpu.VMEM((rows, EDGE_NODE), BF16),
            pltpu.VMEM(pair_feats.shape, BF16),
            pltpu.VMEM(w_qkv.shape[::-1], BF16),
            pltpu.VMEM(w_points.shape[::-1], BF16),
            pltpu.VMEM(w_out.shape, BF16),
            pltpu.VMEM(w_trans.shape, BF16),
            pltpu.VMEM((C_PAIR, w_edge_in.shape[1]), BF16),
            pltpu.VMEM((rows, count, w_edge_in.shape[1]), BF16),
            pltpu.VMEM((lines, count), F32),
            pltpu.VMEM((FRAME, FRAME), F32),
            pltpu.VMEM((4, WIDTH, d_node), BF16),
            pltpu.VMEM((lines, C_PAIR), F32),
            pltpu.SemaphoreType.DMA((7,)),
            pltpu.SemaphoreType.DMA((n,)),
            pltpu.SemaphoreType.DMA((n,)),
            pltpu.SemaphoreType.DMA((n,)),
            pltpu.SemaphoreType.DMA((n,)),
        ],
        compiler_params=pltpu.CompilerParams(
            collective_id=0, has_side_effects=True, vmem_limit_bytes=VMEM_LIMIT
        ),
        name="node",
    )(
        node_feats,
        trans.T,
        frame_seed.T,
        mask_line,
        chain_index[None],
        w_bias.T,
        head_weights[None],
        chain_bias[None],
        b_out[None],
        w_edge_node,
        pair_feats,
        w_qkv.T,
        w_points.T,
        w_out,
        w_trans,
        w_edge_in,
    )
    step_rows = 2 if count <= 512 else 1

    def fixed(array):
        return pl.BlockSpec(array.shape, lambda s: (0,) * array.ndim)

    constants = (
        ends,
        own,
        nodes,
        mask_line,
        w_edge_in,
        b_edge_in,
        w_edge_mid,
        b_edge_mid,
        w_edge_out,
        b_edge_out[None],
    )
    block = pl.BlockSpec((step_rows, count, C_PAIR), lambda s: (s, 0, 0))
    wide_block = pl.BlockSpec((step_rows,) + pre.shape[1:], lambda s: (s, 0, 0))
    return pl.pallas_call(
        functools.partial(edge_kernel, step_rows),
        out_shape=(
            jax.ShapeDtypeStruct((rows, d_node), BF16),
            jax.ShapeDtypeStruct(pair_feats.shape, BF16),
        ),
        grid=(rows // step_rows,),
        in_specs=[block, wide_block] + [fixed(array) for array in constants],
        out_specs=(fixed(nodes), block),
        scratch_shapes=[
            pltpu.VMEM((rows, w_edge_in.shape[1]), F32),
            pltpu.VMEM((count, C_PAIR), F32),
            pltpu.VMEM((count, w_edge_in.shape[1]), F32),
        ],
        compiler_params=pltpu.CompilerParams(vmem_limit_bytes=VMEM_LIMIT),
        name="edge",
    )(pair_feats, pre, *constants)


def solution(mesh):
    split = P(("grp", "row"), None)
    in_specs = (
        split,
        P(("grp", "row"), None, None),
        split,
        split,
        P("grp"),
        P("grp"),
    ) + (P(),) * 15
    out_specs = (split, P(("grp", "row"), None, None))
    return jax.shard_map(
        functools.partial(body, mesh.shape["row"]),
        mesh=mesh,
        in_specs=in_specs,
        out_specs=out_specs,
        check_vma=False,
    )
```

```python
import functools
import math

import jax
import jax.numpy as jnp
from jax import lax
from jax.experimental import pallas as pl
from jax.experimental.pallas import tpu as pltpu
from jax.sharding import PartitionSpec as P

C_PAIR = 128
HEADS = 12
HEAD_DIM = 16
QK_POINTS = 4
V_POINTS = 8
POINTS = 2 * QK_POINTS + V_POINTS
EDGE_NODE = 128
WIDTH = HEADS * HEAD_DIM
PACK = 16
FRAME = 128

mask_bias = 100000.0
norm_eps = 1e-05
point_eps = 1e-08
F32 = jnp.float32
BF16 = jnp.bfloat16
MESH = pl.DeviceIdType.MESH
VMEM_LIMIT = 60 << 20


def dot(a, b):
    return jnp.dot(a, b, preferred_element_type=F32)


def dot_nt(a, b):
    return lax.dot_general(a, b, (((1,), (1,)), ((), ())), preferred_element_type=F32)


def layer_norm(values):
    centred = values - jnp.mean(values, -1, keepdims=True)
    return centred * lax.rsqrt(jnp.mean(centred * centred, -1, keepdims=True) + norm_eps)


def cos_sin(steps):
    quarter = jnp.floor((steps + 32.0) * (1.0 / 64.0))
    x = (steps - 64.0 * quarter) * (2.0 * math.pi / 256.0)
    y = x * x
    c = 1.0 + y * (-0.5 + y * (1 / 24 + y * (-1 / 720 + y * (1 / 40320 - y * (1 / 3628800)))))
    s = x * (1.0 + y * (-1 / 6 + y * (1 / 120 + y * (-1 / 5040 + y * (1 / 362880)))))
    one, two, three = quarter == 1.0, quarter == 2.0, quarter == 3.0
    cosine = jnp.where(one, -s, jnp.where(two, -c, jnp.where(three, s, c)))
    sine = jnp.where(one, c, jnp.where(two, -s, jnp.where(three, -c, s)))
    return cosine, sine


def frames(frame):
    cosine, sine = cos_sin(frame)
    c0, c1, c2 = (cosine[:, k : k + 1] for k in (3, 4, 5))
    s0, s1, s2 = (sine[:, k : k + 1] for k in (3, 4, 5))
    rotate = (
        (c0 * c1 * c2 - s0 * s2, -c0 * c1 * s2 - s0 * c2, c0 * s1),
        (s0 * c1 * c2 + c0 * s2, c0 * c2 - s0 * c1 * s2, s0 * s1),
        (-s1 * c2, s1 * s2, c1),
    )
    return rotate, tuple(frame[:, k : k + 1] for k in range(3))


def spatial_points(nodes, rotate, trans, w_points):
    local = [dot_nt(nodes, w_points[b * WIDTH : (b + 1) * WIDTH, :]) for b in range(3)]
    return [
        (
            rotate[a][0] * local[0] + rotate[a][1] * local[1] + rotate[a][2] * local[2] + trans[a]
        ).astype(BF16)
        for a in range(3)
    ]


def iota(shape, axis):
    return lax.broadcasted_iota(jnp.int32, shape, axis)


def node_kernel(
    n,
    node_feats,
    trans_ref,
    seed_ref,
    mask_ref,
    chain_ref,
    w_bias,
    head_weights,
    chain_bias,
    b_out,
    w_edge_node,
    pair_hbm,
    w_qkv_hbm,
    w_points_hbm,
    w_out_hbm,
    w_trans_hbm,
    w_in_hbm,
    node_out,
    ends_out,
    own_out,
    pre_hbm,
    packed,
    gathered,
    ends,
    own_end,
    pair,
    w_qkv,
    w_points,
    w_out,
    w_trans,
    w_in,
    pre,
    bias,
    wide,
    w_local,
    pair_part,
    load_sem,
    send_a,
    recv_a,
    send_b,
    recv_b,
):
    me = lax.axis_index("row")
    rows = packed.shape[0]
    count = rows * n
    lines = rows * PACK

    barrier = pltpu.get_barrier_semaphore()

    def greet(s, carry):
        pl.semaphore_signal(
            barrier, inc=1, device_id={"row": lax.rem(me + s, n)}, device_id_type=MESH
        )
        return carry

    lax.fori_loop(1, n, greet, 0)
    loads = [
        pltpu.make_async_copy(src, dst, load_sem.at[k])
        for k, (src, dst) in enumerate(
            (
                (pair_hbm, pair),
                (w_qkv_hbm, w_qkv),
                (w_points_hbm, w_points),
                (w_out_hbm, w_out),
                (w_trans_hbm, w_trans),
                (w_in_hbm.at[pl.ds(0, C_PAIR)], w_in),
            )
        )
    ]
    for load in loads:
        load.start()
    wide[...] = jnp.zeros_like(wide)
    wide[:3, :rows] = trans_ref[...].astype(F32)
    wide[3:6, :rows] = seed_ref[...].astype(F32)
    packed[:, :-FRAME] = node_feats[...]
    packed[:, -FRAME:] = wide[...].T[:rows].astype(BF16)
    wide[:HEADS, :] = w_bias[...].astype(F32)
    wide[HEADS:PACK, :] = jnp.zeros((PACK - HEADS, C_PAIR), F32)
    w_bias_t = wide[:PACK, :].astype(BF16)

    def copy_of(s, src, dst, send, recv):
        return pltpu.make_async_remote_copy(
            src_ref=src,
            dst_ref=dst.at[pl.ds(pl.multiple_of(me * rows, rows), rows)],
            send_sem=send.at[s],
            recv_sem=recv.at[s],
            device_id={"row": lax.rem(me + s, n)},
            device_id_type=MESH,
        )

    def exchange(src, dst, send, recv):
        def go(s, carry):
            copy_of(s, src, dst, send, recv).start()
            return carry

        lax.fori_loop(1, n, go, 0)

    def settle(src, dst, send, recv):
        def go(s, carry):
            copy_of(s, src, dst, send, recv).wait()
            return carry

        lax.fori_loop(1, n, go, 0)

    mine = pl.ds(pl.multiple_of(me * rows, rows), rows)
    gathered[mine, :] = packed[...]

    loads[0].wait()

    def bias_row(i, carry):
        bias[pl.ds(pl.multiple_of(i * PACK, PACK), PACK), :] = dot_nt(w_bias_t, pair[i])
        return carry

    lax.fori_loop(0, rows, bias_row, 0, unroll=4)

    line = iota((lines, 1), 0)
    line_head = line % PACK
    line_row = line // PACK
    at_own = iota((lines, count), 1) == me * rows + line_row
    chain_q = jnp.sum(jnp.where(at_own, chain_ref[...], 0), 1, keepdims=True)
    mask_q = jnp.sum(jnp.where(at_own, mask_ref[...], 0), 1, keepdims=True)
    at_head = iota((lines, HEADS), 1) == line_head
    gamma = jnp.sum(jnp.where(at_head, jax.nn.softplus(head_weights[...]), 0.0), 1, keepdims=True)
    chain_add = jnp.sum(jnp.where(at_head, chain_bias[...], 0.0), 1, keepdims=True)
    column = iota((lines, WIDTH), 1)
    of_head = column // HEAD_DIM == line_head
    of_key = of_head & (column % POINTS >= QK_POINTS) & (column % POINTS < 2 * QK_POINTS)
    of_value = of_head & (column % POINTS >= 2 * QK_POINTS)
    spread = (iota((lines, rows), 1) == line_row).astype(BF16)
    same = (chain_q == chain_ref[...]).astype(F32)
    pair_mask = (mask_q * mask_ref[...]).astype(F32)
    bias[...] = bias[...] * math.sqrt(1.0 / 3.0) + (
        chain_add * same + mask_bias * (pair_mask - 1.0)
    )

    loads[1].wait()
    loads[2].wait()
    nodes = packed[:, :-FRAME]
    rotate, trans = frames(packed[:, -FRAME:].astype(F32))
    query = dot_nt(nodes, w_qkv[:WIDTH, :]).astype(BF16)
    own_points = spatial_points(nodes, rotate, trans, w_points)
    q_lines = jnp.where(of_head, dot(spread, query), 0.0).astype(BF16)
    p_lines = [
        jnp.where(of_key, pltpu.roll(dot(spread, own_points[a]), QK_POINTS, 1), 0.0)
        for a in range(3)
    ]
    q_square = sum(jnp.sum(p * p, 1, keepdims=True) for p in p_lines)
    p_lines = [(-2.0 * p).astype(BF16) for p in p_lines]
    ones_key = of_key.astype(BF16)

    loads[3].wait()
    for k in range(4):
        start = WIDTH + k * HEADS * V_POINTS
        block = w_out[start : start + HEADS * V_POINTS, :].astype(F32)
        block = block.reshape(HEADS, V_POINTS, -1)
        block = jnp.concatenate([jnp.zeros_like(block), block], 1)
        w_local[k] = block.reshape(WIDTH, -1).astype(BF16)

    pl.semaphore_wait(barrier, n - 1)
    partner = me + 1 - 2 * lax.rem(me, 2)

    def across(s):
        return pltpu.make_async_remote_copy(
            src_ref=packed,
            dst_ref=gathered.at[mine],
            send_sem=send_a.at[s],
            recv_sem=recv_a.at[s],
            device_id={"row": lax.rem(me + 2 * s, n)},
            device_id_type=MESH,
        )

    to_partner = pltpu.make_async_remote_copy(
        src_ref=packed,
        dst_ref=gathered.at[mine],
        send_sem=send_a.at[0],
        recv_sem=recv_a.at[0],
        device_id={"row": partner},
        device_id_type=MESH,
    )

    def pass_on(s):
        source = pl.ds(pl.multiple_of(lax.rem(me + n - 2 * s, n) * rows, rows), rows)
        return pltpu.make_async_remote_copy(
            src_ref=gathered.at[source],
            dst_ref=gathered.at[source],
            send_sem=send_a.at[n // 2 + s],
            recv_sem=recv_a.at[n // 2 + s],
            device_id={"row": partner},
            device_id_type=MESH,
        )

    def send_across(s, carry):
        across(s).start()
        return carry

    def relay(s, carry):
        across(s).wait_recv()
        pass_on(s).start()
        return carry

    def finish(s, carry):
        across(s).wait_send()
        pass_on(s).wait()
        return carry

    lax.fori_loop(1, n // 2, send_across, 0)
    to_partner.start()
    loads[5].wait()

    def pair_row(i, carry):
        pre[i] = dot(pair[i], w_in[...]).astype(BF16)
        return carry

    lax.fori_loop(0, rows // 2, pair_row, 0, unroll=2)
    lax.fori_loop(1, n // 2, relay, 0)
    lax.fori_loop(rows // 2, rows, pair_row, 0, unroll=2)
    put_pre = pltpu.make_async_copy(pre, pre_hbm, load_sem.at[6])
    put_pre.start()
    to_partner.wait()
    lax.fori_loop(1, n // 2, finish, 0)

    every = gathered[:, :-FRAME]
    key = dot_nt(every, w_qkv[WIDTH : 2 * WIDTH, :]).astype(BF16)
    value = dot_nt(every, w_qkv[2 * WIDTH :, :]).astype(BF16)
    rotate_all, trans_all = frames(gathered[:, -FRAME:].astype(F32))
    points = spatial_points(every, rotate_all, trans_all, w_points)
    square = sum(p.astype(F32) * p.astype(F32) for p in points)
    high = square.astype(BF16)
    rest = square - high.astype(F32)
    middle = rest.astype(BF16)
    low = (rest - middle.astype(F32)).astype(BF16)
    dots = dot_nt(q_lines, key)
    distance = q_square + (
        dot_nt(p_lines[0], points[0])
        + dot_nt(p_lines[1], points[1])
        + dot_nt(p_lines[2], points[2])
        + dot_nt(ones_key, high)
        + dot_nt(ones_key, middle)
        + dot_nt(ones_key, low)
    )
    weight_c = math.sqrt(2.0 / (9.0 * QK_POINTS))
    third = math.sqrt(1.0 / 3.0)
    logit = (
        dots * (third / math.sqrt(HEAD_DIM)) - (0.5 * weight_c * third) * gamma * distance
    ) + bias[...]
    expo = jnp.exp(logit - jnp.max(logit, 1, keepdims=True))
    inverse = 1.0 / jnp.sum(expo, 1, keepdims=True)
    weights = expo.astype(BF16)

    def collect(lines_value, keep):
        kept = jnp.where(keep, lines_value * inverse, 0.0)
        return jnp.sum(kept.reshape(rows, PACK, WIDTH), 1)

    for i in range(rows):
        part = slice(i * PACK, (i + 1) * PACK)
        pair_part[part, :] = dot(weights[part], pair[i]) * inverse[part]
    node_part = collect(dot(weights, value), of_head)
    shifted = [collect(dot(weights, points[a]), of_value) - trans[a] for a in range(3)]
    local = [
        rotate[0][a] * shifted[0] + rotate[1][a] * shifted[1] + rotate[2][a] * shifted[2]
        for a in range(3)
    ]
    length = jnp.sqrt(
        local[0] * local[0] + local[1] * local[1] + local[2] * local[2] + point_eps
    )
    wide_part = jnp.concatenate(
        [pair_part[pl.ds(h, rows, stride=PACK), :] for h in range(HEADS)], 1
    ).astype(BF16)
    loads[4].wait()
    update = dot(node_part.astype(BF16), w_out[:WIDTH, :]) + b_out[...]
    for k, part in enumerate(local + [length]):
        update = update + dot(part.astype(BF16), w_local[k])
    update = update + dot(wide_part, w_out[WIDTH + 4 * HEADS * V_POINTS :, :])
    first = layer_norm(nodes.astype(F32) + update).astype(BF16)
    hidden = jnp.maximum(dot(first, w_trans[0]), 0.0).astype(BF16)
    hidden = jnp.maximum(dot(hidden, w_trans[1]), 0.0).astype(BF16)
    last = dot(hidden, w_trans[2])
    own_line = iota((rows, count), 1) == me * rows + iota((rows, count), 0)
    own_mask = jnp.sum(jnp.where(own_line, mask_ref[...], 0), 1, keepdims=True)
    result = (layer_norm(first.astype(F32) + last) * own_mask.astype(F32)).astype(BF16)
    own_end[...] = dot(result, w_edge_node[...]).astype(BF16)
    exchange(own_end, ends, send_b, recv_b)
    node_out[...] = result
    own_out[...] = own_end[...].astype(F32)
    ends[mine, :] = own_end[...]
    settle(own_end, ends, send_b, recv_b)
    ends_out[...] = ends[...]
    put_pre.wait()


def edge_kernel(
    step_rows,
    pair,
    pre0,
    ends,
    own,
    nodes,
    mask_ref,
    w_in,
    b_in,
    w_mid,
    b_mid,
    w_last,
    b_last,
    node_out,
    out,
    near,
    mask_cols,
    far_in,
):
    me = lax.axis_index("row")
    step = pl.program_id(0)
    count = ends.shape[0]
    rows = own.shape[0]
    c = C_PAIR

    @pl.when(step == 0)
    def _():
        near[...] = dot(own[...].astype(BF16), w_in[c : c + EDGE_NODE, :]) + b_in[...][None, :]
        node_out[...] = nodes[...]
        eye = iota((count, count), 0) == iota((count, count), 1)
        line = jnp.sum(jnp.where(eye, mask_ref[...], 0), 1, keepdims=True).astype(F32)
        mask_cols[...] = jnp.broadcast_to(line, mask_cols.shape)
        far_in[...] = dot(ends[...], w_in[c + EDGE_NODE :, :])

    far = ends[...]
    for r in range(step_rows):
        i = step * step_rows + r
        row = pair[r]
        near_row = near[pl.ds(i, 1), :]
        own_row = own[pl.ds(i, 1), :]
        mask_row = mask_cols[pl.ds(me * rows + i, 1), :]
        pre = pre0[r].astype(F32) + (far_in[...] + near_row)
        first = jnp.maximum(pre.astype(BF16), 0.0)
        second = jnp.maximum(dot(first, w_mid[...]) + b_mid[...][None, :], 0.0)
        resid = jnp.concatenate(
            [
                second[:, :c] + row.astype(F32),
                second[:, c : c + EDGE_NODE] + own_row,
                second[:, c + EDGE_NODE :] + far.astype(F32),
            ],
            1,
        ).astype(BF16)
        last = dot(resid, w_last[...]) + b_last[...]
        out[r] = (layer_norm(last) * (mask_row * mask_cols[...])).astype(BF16)


def body(
    n,
    node_feats,
    pair_feats,
    trans,
    frame_seed,
    residue_mask,
    chain_index,
    w_qkv,
    w_points,
    w_bias,
    head_weights,
    chain_bias,
    w_out,
    b_out,
    w_trans,
    w_edge_node,
    w_edge_in,
    b_edge_in,
    w_edge_mid,
    b_edge_mid,
    w_edge_out,
    b_edge_out,
):
    rows, d_node = node_feats.shape
    count = rows * n
    lines = rows * PACK
    mask_line = residue_mask[None]
    vmem = pl.BlockSpec(memory_space=pltpu.VMEM)
    hbm = pl.BlockSpec(memory_space=pl.ANY)
    nodes, ends, own, pre = pl.pallas_call(
        functools.partial(node_kernel, n),
        out_shape=(
            jax.ShapeDtypeStruct((rows, d_node), BF16),
            jax.ShapeDtypeStruct((count, EDGE_NODE), BF16),
            jax.ShapeDtypeStruct((rows, EDGE_NODE), F32),
            jax.ShapeDtypeStruct((rows, count, w_edge_in.shape[1]), BF16),
        ),
        in_specs=[vmem] * 10 + [hbm] * 6,
        out_specs=(vmem, vmem, vmem, hbm),
        scratch_shapes=[
            pltpu.VMEM((rows, d_node + FRAME), BF16),
            pltpu.VMEM((count, d_node + FRAME), BF16),
            pltpu.VMEM((count, EDGE_NODE), BF16),
            pltpu.VMEM((rows, EDGE_NODE), BF16),
            pltpu.VMEM(pair_feats.shape, BF16),
            pltpu.VMEM(w_qkv.shape[::-1], BF16),
            pltpu.VMEM(w_points.shape[::-1], BF16),
            pltpu.VMEM(w_out.shape, BF16),
            pltpu.VMEM(w_trans.shape, BF16),
            pltpu.VMEM((C_PAIR, w_edge_in.shape[1]), BF16),
            pltpu.VMEM((rows, count, w_edge_in.shape[1]), BF16),
            pltpu.VMEM((lines, count), F32),
            pltpu.VMEM((FRAME, FRAME), F32),
            pltpu.VMEM((4, WIDTH, d_node), BF16),
            pltpu.VMEM((lines, C_PAIR), F32),
            pltpu.SemaphoreType.DMA((7,)),
            pltpu.SemaphoreType.DMA((n,)),
            pltpu.SemaphoreType.DMA((n,)),
            pltpu.SemaphoreType.DMA((n,)),
            pltpu.SemaphoreType.DMA((n,)),
        ],
        compiler_params=pltpu.CompilerParams(
            collective_id=0, has_side_effects=True, vmem_limit_bytes=VMEM_LIMIT
        ),
        name="node",
    )(
        node_feats,
        trans.T,
        frame_seed.T,
        mask_line,
        chain_index[None],
        w_bias.T,
        head_weights[None],
        chain_bias[None],
        b_out[None],
        w_edge_node,
        pair_feats,
        w_qkv.T,
        w_points.T,
        w_out,
        w_trans,
        w_edge_in,
    )
    step_rows = 4 if count <= 512 else 1

    def fixed(array):
        return pl.BlockSpec(array.shape, lambda s: (0,) * array.ndim)

    constants = (
        ends,
        own,
        nodes,
        mask_line,
        w_edge_in,
        b_edge_in,
        w_edge_mid,
        b_edge_mid,
        w_edge_out,
        b_edge_out[None],
    )
    block = pl.BlockSpec((step_rows, count, C_PAIR), lambda s: (s, 0, 0))
    wide_block = pl.BlockSpec((step_rows,) + pre.shape[1:], lambda s: (s, 0, 0))
    return pl.pallas_call(
        functools.partial(edge_kernel, step_rows),
        out_shape=(
            jax.ShapeDtypeStruct((rows, d_node), BF16),
            jax.ShapeDtypeStruct(pair_feats.shape, BF16),
        ),
        grid=(rows // step_rows,),
        in_specs=[block, wide_block] + [fixed(array) for array in constants],
        out_specs=(fixed(nodes), block),
        scratch_shapes=[
            pltpu.VMEM((rows, w_edge_in.shape[1]), F32),
            pltpu.VMEM((count, C_PAIR), F32),
            pltpu.VMEM((count, w_edge_in.shape[1]), F32),
        ],
        compiler_params=pltpu.CompilerParams(vmem_limit_bytes=VMEM_LIMIT),
        name="edge",
    )(pair_feats, pre, *constants)


def solution(mesh):
    split = P(("grp", "row"), None)
    in_specs = (
        split,
        P(("grp", "row"), None, None),
        split,
        split,
        P("grp"),
        P("grp"),
    ) + (P(),) * 15
    out_specs = (split, P(("grp", "row"), None, None))
    return jax.shard_map(
        functools.partial(body, mesh.shape["row"]),
        mesh=mesh,
        in_specs=in_specs,
        out_specs=out_specs,
        check_vma=False,
    )
```

```python
import functools
import math

import jax
import jax.numpy as jnp
from jax import lax
from jax.experimental import pallas as pl
from jax.experimental.pallas import tpu as pltpu
from jax.sharding import PartitionSpec as P

C_PAIR = 128
HEADS = 12
HEAD_DIM = 16
QK_POINTS = 4
V_POINTS = 8
POINTS = 2 * QK_POINTS + V_POINTS
EDGE_NODE = 128
WIDTH = HEADS * HEAD_DIM
PACK = 16
FRAME = 128

mask_bias = 100000.0
norm_eps = 1e-05
point_eps = 1e-08
F32 = jnp.float32
BF16 = jnp.bfloat16
MESH = pl.DeviceIdType.MESH
VMEM_LIMIT = 60 << 20


def dot(a, b):
    return jnp.dot(a, b, preferred_element_type=F32)


def dot_nt(a, b):
    return lax.dot_general(a, b, (((1,), (1,)), ((), ())), preferred_element_type=F32)


def layer_norm(values):
    centred = values - jnp.mean(values, -1, keepdims=True)
    return centred * lax.rsqrt(jnp.mean(centred * centred, -1, keepdims=True) + norm_eps)


def cos_sin(steps):
    quarter = jnp.floor((steps + 32.0) * (1.0 / 64.0))
    x = (steps - 64.0 * quarter) * (2.0 * math.pi / 256.0)
    y = x * x
    c = 1.0 + y * (-0.5 + y * (1 / 24 + y * (-1 / 720 + y * (1 / 40320 - y * (1 / 3628800)))))
    s = x * (1.0 + y * (-1 / 6 + y * (1 / 120 + y * (-1 / 5040 + y * (1 / 362880)))))
    one, two, three = quarter == 1.0, quarter == 2.0, quarter == 3.0
    cosine = jnp.where(one, -s, jnp.where(two, -c, jnp.where(three, s, c)))
    sine = jnp.where(one, c, jnp.where(two, -s, jnp.where(three, -c, s)))
    return cosine, sine


def frames(frame):
    cosine, sine = cos_sin(frame)
    c0, c1, c2 = (cosine[:, k : k + 1] for k in (3, 4, 5))
    s0, s1, s2 = (sine[:, k : k + 1] for k in (3, 4, 5))
    rotate = (
        (c0 * c1 * c2 - s0 * s2, -c0 * c1 * s2 - s0 * c2, c0 * s1),
        (s0 * c1 * c2 + c0 * s2, c0 * c2 - s0 * c1 * s2, s0 * s1),
        (-s1 * c2, s1 * s2, c1),
    )
    return rotate, tuple(frame[:, k : k + 1] for k in range(3))


def spatial_points(nodes, rotate, trans, w_points):
    local = [dot_nt(nodes, w_points[b * WIDTH : (b + 1) * WIDTH, :]) for b in range(3)]
    return [
        (
            rotate[a][0] * local[0] + rotate[a][1] * local[1] + rotate[a][2] * local[2] + trans[a]
        ).astype(BF16)
        for a in range(3)
    ]


def iota(shape, axis):
    return lax.broadcasted_iota(jnp.int32, shape, axis)


def node_kernel(
    n,
    node_feats,
    trans_ref,
    seed_ref,
    mask_ref,
    chain_ref,
    w_bias,
    head_weights,
    chain_bias,
    b_out,
    w_edge_node,
    pair_hbm,
    w_qkv_hbm,
    w_points_hbm,
    w_out_hbm,
    w_trans_hbm,
    w_in_hbm,
    node_out,
    ends_out,
    own_out,
    pre_hbm,
    packed,
    gathered,
    ends,
    own_end,
    pair,
    w_qkv,
    w_points,
    w_out,
    w_trans,
    w_in,
    pre,
    bias,
    wide,
    w_local,
    pair_part,
    load_sem,
    send_a,
    recv_a,
    send_b,
    recv_b,
):
    me = lax.axis_index("row")
    rows = packed.shape[0]
    count = rows * n
    lines = rows * PACK

    barrier = pltpu.get_barrier_semaphore()

    def greet(s, carry):
        pl.semaphore_signal(
            barrier, inc=1, device_id={"row": lax.rem(me + s, n)}, device_id_type=MESH
        )
        return carry

    lax.fori_loop(1, n, greet, 0)
    loads = [
        pltpu.make_async_copy(src, dst, load_sem.at[k])
        for k, (src, dst) in enumerate(
            (
                (pair_hbm, pair),
                (w_qkv_hbm, w_qkv),
                (w_points_hbm, w_points),
                (w_out_hbm, w_out),
                (w_trans_hbm, w_trans),
                (w_in_hbm.at[pl.ds(0, C_PAIR)], w_in),
            )
        )
    ]
    for load in loads:
        load.start()
    wide[...] = jnp.zeros_like(wide)
    wide[:3, :rows] = trans_ref[...].astype(F32)
    wide[3:6, :rows] = seed_ref[...].astype(F32)
    packed[:, :-FRAME] = node_feats[...]
    packed[:, -FRAME:] = wide[...].T[:rows].astype(BF16)
    wide[:HEADS, :] = w_bias[...].astype(F32)
    wide[HEADS:PACK, :] = jnp.zeros((PACK - HEADS, C_PAIR), F32)
    w_bias_t = wide[:PACK, :].astype(BF16)

    def copy_of(s, src, dst, send, recv):
        return pltpu.make_async_remote_copy(
            src_ref=src,
            dst_ref=dst.at[pl.ds(pl.multiple_of(me * rows, rows), rows)],
            send_sem=send.at[s],
            recv_sem=recv.at[s],
            device_id={"row": lax.rem(me + s, n)},
            device_id_type=MESH,
        )

    def exchange(src, dst, send, recv):
        def go(s, carry):
            copy_of(s, src, dst, send, recv).start()
            return carry

        lax.fori_loop(1, n, go, 0)

    def settle(src, dst, send, recv):
        def go(s, carry):
            copy_of(s, src, dst, send, recv).wait()
            return carry

        lax.fori_loop(1, n, go, 0)

    mine = pl.ds(pl.multiple_of(me * rows, rows), rows)
    gathered[mine, :] = packed[...]

    loads[0].wait()

    def bias_row(i, carry):
        bias[pl.ds(pl.multiple_of(i * PACK, PACK), PACK), :] = dot_nt(w_bias_t, pair[i])
        return carry

    lax.fori_loop(0, rows, bias_row, 0, unroll=4)

    line = iota((lines, 1), 0)
    line_head = line % PACK
    line_row = line // PACK
    at_own = iota((lines, count), 1) == me * rows + line_row
    chain_q = jnp.sum(jnp.where(at_own, chain_ref[...], 0), 1, keepdims=True)
    mask_q = jnp.sum(jnp.where(at_own, mask_ref[...], 0), 1, keepdims=True)
    at_head = iota((lines, HEADS), 1) == line_head
    gamma = jnp.sum(jnp.where(at_head, jax.nn.softplus(head_weights[...]), 0.0), 1, keepdims=True)
    chain_add = jnp.sum(jnp.where(at_head, chain_bias[...], 0.0), 1, keepdims=True)
    column = iota((lines, WIDTH), 1)
    of_head = column // HEAD_DIM == line_head
    of_key = of_head & (column % POINTS >= QK_POINTS) & (column % POINTS < 2 * QK_POINTS)
    of_value = of_head & (column % POINTS >= 2 * QK_POINTS)
    spread = (iota((lines, rows), 1) == line_row).astype(BF16)
    same = (chain_q == chain_ref[...]).astype(F32)
    pair_mask = (mask_q * mask_ref[...]).astype(F32)
    bias[...] = bias[...] * math.sqrt(1.0 / 3.0) + (
        chain_add * same + mask_bias * (pair_mask - 1.0)
    )

    pl.semaphore_wait(barrier, n - 1)
    partner = me + 1 - 2 * lax.rem(me, 2)

    def across(s):
        return pltpu.make_async_remote_copy(
            src_ref=packed,
            dst_ref=gathered.at[mine],
            send_sem=send_a.at[s],
            recv_sem=recv_a.at[s],
            device_id={"row": lax.rem(me + 2 * s, n)},
            device_id_type=MESH,
        )

    to_partner = pltpu.make_async_remote_copy(
        src_ref=packed,
        dst_ref=gathered.at[mine],
        send_sem=send_a.at[0],
        recv_sem=recv_a.at[0],
        device_id={"row": partner},
        device_id_type=MESH,
    )

    def pass_on(s):
        source = pl.ds(pl.multiple_of(lax.rem(me + n - 2 * s, n) * rows, rows), rows)
        return pltpu.make_async_remote_copy(
            src_ref=gathered.at[source],
            dst_ref=gathered.at[source],
            send_sem=send_a.at[n // 2 + s],
            recv_sem=recv_a.at[n // 2 + s],
            device_id={"row": partner},
            device_id_type=MESH,
        )

    def send_across(s, carry):
        across(s).start()
        return carry

    def relay(s, carry):
        across(s).wait_recv()
        pass_on(s).start()
        return carry

    def finish(s, carry):
        across(s).wait_send()
        pass_on(s).wait()
        return carry

    lax.fori_loop(1, n // 2, send_across, 0)
    to_partner.start()

    loads[1].wait()
    loads[2].wait()
    nodes = packed[:, :-FRAME]
    rotate, trans = frames(packed[:, -FRAME:].astype(F32))
    query = dot_nt(nodes, w_qkv[:WIDTH, :]).astype(BF16)
    own_points = spatial_points(nodes, rotate, trans, w_points)
    q_lines = jnp.where(of_head, dot(spread, query), 0.0).astype(BF16)
    p_lines = [
        jnp.where(of_key, pltpu.roll(dot(spread, own_points[a]), QK_POINTS, 1), 0.0)
        for a in range(3)
    ]
    q_square = sum(jnp.sum(p * p, 1, keepdims=True) for p in p_lines)
    p_lines = [(-2.0 * p).astype(BF16) for p in p_lines]
    ones_key = of_key.astype(BF16)

    loads[3].wait()
    for k in range(4):
        start = WIDTH + k * HEADS * V_POINTS
        block = w_out[start : start + HEADS * V_POINTS, :].astype(F32)
        block = block.reshape(HEADS, V_POINTS, -1)
        block = jnp.concatenate([jnp.zeros_like(block), block], 1)
        w_local[k] = block.reshape(WIDTH, -1).astype(BF16)

    loads[5].wait()

    def pair_row(i, carry):
        pre[i] = dot(pair[i], w_in[...]).astype(BF16)
        return carry

    half = rows // 2
    puts = [
        pltpu.make_async_copy(
            pre.at[pl.ds(k * half, half)], pre_hbm.at[pl.ds(k * half, half)], load_sem.at[6 + k]
        )
        for k in range(2)
    ]
    lax.fori_loop(1, n // 2, relay, 0)
    lax.fori_loop(0, half, pair_row, 0, unroll=2)
    puts[0].start()
    to_partner.wait()
    lax.fori_loop(1, n // 2, finish, 0)

    every = gathered[:, :-FRAME]
    key = dot_nt(every, w_qkv[WIDTH : 2 * WIDTH, :]).astype(BF16)
    value = dot_nt(every, w_qkv[2 * WIDTH :, :]).astype(BF16)
    rotate_all, trans_all = frames(gathered[:, -FRAME:].astype(F32))
    points = spatial_points(every, rotate_all, trans_all, w_points)
    square = sum(p.astype(F32) * p.astype(F32) for p in points)
    high = square.astype(BF16)
    rest = square - high.astype(F32)
    middle = rest.astype(BF16)
    low = (rest - middle.astype(F32)).astype(BF16)
    dots = dot_nt(q_lines, key)
    distance = q_square + (
        dot_nt(p_lines[0], points[0])
        + dot_nt(p_lines[1], points[1])
        + dot_nt(p_lines[2], points[2])
        + dot_nt(ones_key, high)
        + dot_nt(ones_key, middle)
        + dot_nt(ones_key, low)
    )
    weight_c = math.sqrt(2.0 / (9.0 * QK_POINTS))
    third = math.sqrt(1.0 / 3.0)
    logit = (
        dots * (third / math.sqrt(HEAD_DIM)) - (0.5 * weight_c * third) * gamma * distance
    ) + bias[...]
    expo = jnp.exp(logit - jnp.max(logit, 1, keepdims=True))
    inverse = 1.0 / jnp.sum(expo, 1, keepdims=True)
    weights = expo.astype(BF16)

    def collect(lines_value, keep):
        kept = jnp.where(keep, lines_value * inverse, 0.0)
        return jnp.sum(kept.reshape(rows, PACK, WIDTH), 1)

    for i in range(rows):
        part = slice(i * PACK, (i + 1) * PACK)
        pair_part[part, :] = dot(weights[part], pair[i]) * inverse[part]
    node_part = collect(dot(weights, value), of_head)
    shifted = [collect(dot(weights, points[a]), of_value) - trans[a] for a in range(3)]
    local = [
        rotate[0][a] * shifted[0] + rotate[1][a] * shifted[1] + rotate[2][a] * shifted[2]
        for a in range(3)
    ]
    length = jnp.sqrt(
        local[0] * local[0] + local[1] * local[1] + local[2] * local[2] + point_eps
    )
    wide_part = jnp.concatenate(
        [pair_part[pl.ds(h, rows, stride=PACK), :] for h in range(HEADS)], 1
    ).astype(BF16)
    loads[4].wait()
    update = dot(node_part.astype(BF16), w_out[:WIDTH, :]) + b_out[...]
    for k, part in enumerate(local + [length]):
        update = update + dot(part.astype(BF16), w_local[k])
    update = update + dot(wide_part, w_out[WIDTH + 4 * HEADS * V_POINTS :, :])
    first = layer_norm(nodes.astype(F32) + update).astype(BF16)
    hidden = jnp.maximum(dot(first, w_trans[0]), 0.0).astype(BF16)
    hidden = jnp.maximum(dot(hidden, w_trans[1]), 0.0).astype(BF16)
    last = dot(hidden, w_trans[2])
    own_line = iota((rows, count), 1) == me * rows + iota((rows, count), 0)
    own_mask = jnp.sum(jnp.where(own_line, mask_ref[...], 0), 1, keepdims=True)
    result = (layer_norm(first.astype(F32) + last) * own_mask.astype(F32)).astype(BF16)
    own_end[...] = dot(result, w_edge_node[...]).astype(BF16)
    exchange(own_end, ends, send_b, recv_b)
    node_out[...] = result
    lax.fori_loop(half, rows, pair_row, 0, unroll=2)
    puts[1].start()
    own_out[...] = own_end[...].astype(F32)
    ends[mine, :] = own_end[...]
    settle(own_end, ends, send_b, recv_b)
    ends_out[...] = ends[...]
    puts[0].wait()
    puts[1].wait()


def edge_kernel(
    step_rows,
    pair,
    pre0,
    ends,
    own,
    nodes,
    mask_ref,
    w_in,
    b_in,
    w_mid,
    b_mid,
    w_last,
    b_last,
    node_out,
    out,
    near,
    mask_cols,
    far_in,
):
    me = lax.axis_index("row")
    step = pl.program_id(0)
    count = ends.shape[0]
    rows = own.shape[0]
    c = C_PAIR

    @pl.when(step == 0)
    def _():
        near[...] = dot(own[...].astype(BF16), w_in[c : c + EDGE_NODE, :]) + b_in[...][None, :]
        node_out[...] = nodes[...]
        eye = iota((count, count), 0) == iota((count, count), 1)
        line = jnp.sum(jnp.where(eye, mask_ref[...], 0), 1, keepdims=True).astype(F32)
        mask_cols[...] = jnp.broadcast_to(line, mask_cols.shape)
        far_in[...] = dot(ends[...], w_in[c + EDGE_NODE :, :])

    far = ends[...]
    for r in range(step_rows):
        i = step * step_rows + r
        row = pair[r]
        near_row = near[pl.ds(i, 1), :]
        own_row = own[pl.ds(i, 1), :]
        mask_row = mask_cols[pl.ds(me * rows + i, 1), :]
        pre = pre0[r].astype(F32) + (far_in[...] + near_row)
        first = jnp.maximum(pre.astype(BF16), 0.0)
        second = jnp.maximum(dot(first, w_mid[...]) + b_mid[...][None, :], 0.0)
        resid = jnp.concatenate(
            [
                second[:, :c] + row.astype(F32),
                second[:, c : c + EDGE_NODE] + own_row,
                second[:, c + EDGE_NODE :] + far.astype(F32),
            ],
            1,
        ).astype(BF16)
        last = dot(resid, w_last[...]) + b_last[...]
        out[r] = (layer_norm(last) * (mask_row * mask_cols[...])).astype(BF16)


def body(
    n,
    node_feats,
    pair_feats,
    trans,
    frame_seed,
    residue_mask,
    chain_index,
    w_qkv,
    w_points,
    w_bias,
    head_weights,
    chain_bias,
    w_out,
    b_out,
    w_trans,
    w_edge_node,
    w_edge_in,
    b_edge_in,
    w_edge_mid,
    b_edge_mid,
    w_edge_out,
    b_edge_out,
):
    rows, d_node = node_feats.shape
    count = rows * n
    lines = rows * PACK
    mask_line = residue_mask[None]
    vmem = pl.BlockSpec(memory_space=pltpu.VMEM)
    hbm = pl.BlockSpec(memory_space=pl.ANY)
    nodes, ends, own, pre = pl.pallas_call(
        functools.partial(node_kernel, n),
        out_shape=(
            jax.ShapeDtypeStruct((rows, d_node), BF16),
            jax.ShapeDtypeStruct((count, EDGE_NODE), BF16),
            jax.ShapeDtypeStruct((rows, EDGE_NODE), F32),
            jax.ShapeDtypeStruct((rows, count, w_edge_in.shape[1]), BF16),
        ),
        in_specs=[vmem] * 10 + [hbm] * 6,
        out_specs=(vmem, vmem, vmem, hbm),
        scratch_shapes=[
            pltpu.VMEM((rows, d_node + FRAME), BF16),
            pltpu.VMEM((count, d_node + FRAME), BF16),
            pltpu.VMEM((count, EDGE_NODE), BF16),
            pltpu.VMEM((rows, EDGE_NODE), BF16),
            pltpu.VMEM(pair_feats.shape, BF16),
            pltpu.VMEM(w_qkv.shape[::-1], BF16),
            pltpu.VMEM(w_points.shape[::-1], BF16),
            pltpu.VMEM(w_out.shape, BF16),
            pltpu.VMEM(w_trans.shape, BF16),
            pltpu.VMEM((C_PAIR, w_edge_in.shape[1]), BF16),
            pltpu.VMEM((rows, count, w_edge_in.shape[1]), BF16),
            pltpu.VMEM((lines, count), F32),
            pltpu.VMEM((FRAME, FRAME), F32),
            pltpu.VMEM((4, WIDTH, d_node), BF16),
            pltpu.VMEM((lines, C_PAIR), F32),
            pltpu.SemaphoreType.DMA((8,)),
            pltpu.SemaphoreType.DMA((n,)),
            pltpu.SemaphoreType.DMA((n,)),
            pltpu.SemaphoreType.DMA((n,)),
            pltpu.SemaphoreType.DMA((n,)),
        ],
        compiler_params=pltpu.CompilerParams(
            collective_id=0, has_side_effects=True, vmem_limit_bytes=VMEM_LIMIT
        ),
        name="node",
    )(
        node_feats,
        trans.T,
        frame_seed.T,
        mask_line,
        chain_index[None],
        w_bias.T,
        head_weights[None],
        chain_bias[None],
        b_out[None],
        w_edge_node,
        pair_feats,
        w_qkv.T,
        w_points.T,
        w_out,
        w_trans,
        w_edge_in,
    )
    step_rows = 4 if count <= 512 else 1

    def fixed(array):
        return pl.BlockSpec(array.shape, lambda s: (0,) * array.ndim)

    constants = (
        ends,
        own,
        nodes,
        mask_line,
        w_edge_in,
        b_edge_in,
        w_edge_mid,
        b_edge_mid,
        w_edge_out,
        b_edge_out[None],
    )
    block = pl.BlockSpec((step_rows, count, C_PAIR), lambda s: (s, 0, 0))
    wide_block = pl.BlockSpec((step_rows,) + pre.shape[1:], lambda s: (s, 0, 0))
    return pl.pallas_call(
        functools.partial(edge_kernel, step_rows),
        out_shape=(
            jax.ShapeDtypeStruct((rows, d_node), BF16),
            jax.ShapeDtypeStruct(pair_feats.shape, BF16),
        ),
        grid=(rows // step_rows,),
        in_specs=[block, wide_block] + [fixed(array) for array in constants],
        out_specs=(fixed(nodes), block),
        scratch_shapes=[
            pltpu.VMEM((rows, w_edge_in.shape[1]), F32),
            pltpu.VMEM((count, C_PAIR), F32),
            pltpu.VMEM((count, w_edge_in.shape[1]), F32),
        ],
        compiler_params=pltpu.CompilerParams(vmem_limit_bytes=VMEM_LIMIT),
        name="edge",
    )(pair_feats, pre, *constants)


def solution(mesh):
    split = P(("grp", "row"), None)
    in_specs = (
        split,
        P(("grp", "row"), None, None),
        split,
        split,
        P("grp"),
        P("grp"),
    ) + (P(),) * 15
    out_specs = (split, P(("grp", "row"), None, None))
    return jax.shard_map(
        functools.partial(body, mesh.shape["row"]),
        mesh=mesh,
        in_specs=in_specs,
        out_specs=out_specs,
        check_vma=False,
    )
```
